32 devices in a mesh: row: 4 (over y, x), col: 8 (over z, core).
Axes of the slice: x: 2, y: 2, z: 4, core: 2. Of those that a mesh axis runs over, the one named last changes fastest.
Arguments:
- positions: float32 [2048, 3, 128], P(('row', 'col')), as said below
- velocities: float32 [2048, 3, 128], P(('row', 'col')), may hold values from -4 to 4
- forces: float32 [2048, 3, 128], P(('row', 'col')), may hold values from -60 to 60
- tiles: int32 [4, 8, 1024, 2], P('row', 'col'), may hold values from 0 to 511, as said below
- counts: int32 [4, 8], P('row', 'col'), may hold values from 1 to 1024, as said below
Outputs:
- moved_positions: float32 [2048, 3, 128], P(('row', 'col'))
- new_velocities: float32 [2048, 3, 128], P(('row', 'col'))
- new_forces: float32 [2048, 3, 128], P(('row', 'col'))
The draws below stay inside these ranges and needn't reach their ends.
Inputs may be any that keep to these rules, and one draw needn't show every extreme that they name: `tiles`: every slot of the list of device (r, c), used or not, holds a pair (li, lj) whose cells are neighbours or equal: li // 64 is c - 1, c or c + 1 modulo 8, lj // 64 is r - 1, r or r + 1 modulo 4, and li % 64 and lj % 64 differ by at most one modulo 64. The slots of one list hold distinct pairs. Entries li lie below 512, entries lj below 256. `counts`: one device's count is exactly 1024. `positions`: each coordinate lies within 0.16 of the matching coordinate of a point of a lattice of spacing 1.2 inside each cell, 4 x 4 x 8 points a cell, one atom at each point.
All inputs are finite; a program needn't handle non-finite values.
Results may differ from the reference program's by a relative error of at most 0.0003.
Values sent between devices are 32-bit elements; how exact they have to be, the bound alone decides.
No kernel may reach another device: no remote copies, remote signals or barrier semaphores. Data moves between devices by JAX's collectives and lax.ppermute only.
A program may use at most 64 MiB of HBM per device.

```python
import jax
import jax.numpy as jnp
from jax import lax

BLK_DEV = 64
TILE_BATCH = 64
TILE_MAX = 1024
NBLOCKS = 2048
N_ROW = 4
N_COL = 8


def draw_positions(key, part):
    atom_ids = jnp.arange(128, dtype=jnp.int32)
    lattice_index = jnp.stack([atom_ids // 32, atom_ids // 8 % 4, atom_ids % 8], axis=0)
    phases = jax.random.randint(jax.random.fold_in(key, 5), (3, 1), 0, 4)
    pattern_table = jnp.array([1.0, 0.0, -1.0, 0.0], jnp.float32)
    pattern = jnp.take(pattern_table, (lattice_index + phases) % 4)
    points = (lattice_index.astype(jnp.float32) + 0.5) * 1.2
    noise_key = jax.random.fold_in(key, 7)
    amplitude = 0.12
    jitter = jax.random.uniform(noise_key, (NBLOCKS, 3, 128), jnp.float32, -0.04, 0.04)
    shaped = points + amplitude * pattern
    return (shaped[None, :, :] + jitter).astype(jnp.float32)


def draw_tiles(key, part):
    candidates = 27 * BLK_DEV
    first_fixed = 13
    second_fixed = (BLK_DEV - 1) * 27 + 13
    own_key = jax.random.fold_in(key, 11)
    keys = jax.random.split(own_key, N_ROW * N_COL)

    def one_list(one_key):
        picked = jax.random.permutation(one_key, candidates - 2)[:TILE_MAX - 2]
        picked = picked + (picked >= first_fixed).astype(picked.dtype)
        picked = picked + (picked >= second_fixed).astype(picked.dtype)
        fixed = jnp.array([first_fixed, second_fixed], dtype=picked.dtype)
        return jnp.concatenate([fixed, picked])
    order = jax.vmap(one_list)(keys)
    order = order.reshape(N_ROW, N_COL, TILE_MAX)
    row_ids = jnp.arange(N_ROW)[:, None, None]
    col_ids = jnp.arange(N_COL)[None, :, None]
    cell_z = order // 27
    rest = order % 27
    step_x = rest % 3 - 1
    step_y = rest // 3 % 3 - 1
    step_z = rest // 9 - 1
    left_ids = (col_ids + step_y) % N_COL * BLK_DEV + cell_z
    right_ids = (row_ids + step_x) % N_ROW * BLK_DEV + (cell_z + step_z) % BLK_DEV
    return jnp.stack([left_ids, right_ids], axis=-1).astype(jnp.int32)


def draw_counts(key, part):
    base_key = jax.random.fold_in(key, 23)
    heavy_key = jax.random.fold_in(key, 29)
    values = jax.random.randint(base_key, (N_ROW * N_COL,), TILE_MAX // 6, TILE_MAX // 2 + 1)
    heavy = jax.random.randint(heavy_key, (), 0, N_ROW * N_COL)
    values = values.at[heavy].set(TILE_MAX)
    return values.reshape(N_ROW, N_COL).astype(jnp.int32)


def shard_levels(stream_key, shape, cuts, smallest, high):
    factor_of = 1.0
    for position, blocks in cuts:
        draws = jax.random.uniform(jax.random.fold_in(jax.random.fold_in(stream_key, 6), position), (blocks,), jnp.float32, smallest / len(cuts), high / len(cuts))
        factor_of = factor_of * jnp.repeat(jnp.exp(draws), shape[position] // blocks).reshape((-1,) + (1,) * (len(shape) - 1 - position))
    return factor_of


def scatter_about(key, dims, spread, reach, shards=(), kind=jnp.bfloat16):
    entries = jax.random.normal(key, dims, jnp.float32) * spread
    if len(shards) > 0:
        entries = shard_levels(key, dims, shards, -0.22, 0.18) * entries
    return jnp.clip(entries, min=-reach, max=reach).astype(kind)


def setup_inputs(seed: int = 0) -> dict:
    splits = jax.random.split(jax.random.key(seed), 6)
    positions = draw_positions(jax.random.fold_in(splits[5], 71), 0)
    velocities = scatter_about(splits[1], (NBLOCKS, 3, 128), 1.0, 4.0, ((0, 32),), jnp.float32)
    forces = scatter_about(splits[2], (NBLOCKS, 3, 128), 10.0, 60.0, ((0, 32),), jnp.float32)
    tiles = draw_tiles(jax.random.fold_in(splits[5], 71), 0)
    counts = draw_counts(jax.random.fold_in(splits[5], 71), 0)
    return {"positions": positions, "velocities": velocities, "forces": forces, "tiles": tiles, "counts": counts}


TIME_STEP = 0.01
CUT_SQ = 6.25
SHIFT_FORCE = 24.0 * (2.0 * 2.5 ** (-13) - 2.5 ** (-7))

def pair_forces(row_atoms, col_atoms, shift):
    separation = row_atoms[:, :, :, None] - col_atoms[:, :, None, :] + shift[:, :, None, None]
    dist_sq = lax.optimization_barrier(jnp.sum(separation * separation, axis=1))
    inside = (dist_sq < CUT_SQ) & (dist_sq > 0.25)
    inv_sq = 1.0 / jnp.where(inside, dist_sq, 1.0)
    inv_six = inv_sq * inv_sq * inv_sq
    magnitude = 24.0 * inv_sq * (2.0 * inv_six * inv_six - inv_six) - SHIFT_FORCE * jnp.sqrt(inv_sq)
    magnitude = jnp.where(inside, magnitude, 0.0)
    return lax.optimization_barrier(jnp.sum(magnitude[:, None, :, :] * separation, axis=3))

def tile_shift(left_ids, right_ids, my_row, my_col, blocks, row_count, col_count):
    cell_y = left_ids // blocks
    cell_zi = left_ids % blocks
    cell_x = right_ids // blocks
    cell_zj = right_ids % blocks
    step_x = (my_row - cell_x + 1) % row_count - 1
    step_y = (cell_y - my_col + 1) % col_count - 1
    step_z = (cell_zi - cell_zj + 1) % blocks - 1
    steps = jnp.stack([step_x, step_y, step_z], axis=-1).astype(jnp.float32)
    return steps * jnp.array([4.8, 4.8, 9.6], jnp.float32)

def reference(positions, velocities, forces, tiles, counts):
    half_vel = velocities + 0.5 * TIME_STEP * forces
    moved = positions + TIME_STEP * half_vel
    flat_tiles = tiles.reshape(N_ROW * N_COL, TILE_MAX, 2)
    flat_counts = counts.reshape(N_ROW * N_COL)

    def per_device(device, total):
        my_row = (device // N_COL).astype(jnp.int32)
        my_col = (device % N_COL).astype(jnp.int32)
        tile_list = flat_tiles[device]
        used = flat_counts[device]

        def per_batch(step_no, acc):
            begin = (step_no * TILE_BATCH).astype(jnp.int32)
            batch = lax.dynamic_slice_in_dim(tile_list, begin, TILE_BATCH, 0)
            left_ids = batch[:, 0]
            right_ids = batch[:, 1]
            shift = tile_shift(left_ids, right_ids, my_row, my_col, BLK_DEV, N_ROW, N_COL)
            global_i = my_row * N_COL * BLK_DEV + left_ids
            global_j = (right_ids // BLK_DEV * N_COL + my_col) * BLK_DEV + right_ids % BLK_DEV
            alive = begin + jnp.arange(TILE_BATCH, dtype=jnp.int32) < used
            pair_force = pair_forces(moved[global_i], moved[global_j], shift)
            pair_force = jnp.where(alive[:, None, None], pair_force, 0.0)
            return acc.at[global_i].add(pair_force)
        return lax.fori_loop(0, (used + TILE_BATCH - 1) // TILE_BATCH, per_batch, total)
    start = jnp.zeros((NBLOCKS, 3, 128), jnp.float32)
    new_forces = lax.fori_loop(0, N_ROW * N_COL, per_device, start)
    new_velocities = half_vel + 0.5 * TIME_STEP * new_forces
    return (moved, new_velocities, new_forces)
```

```python
import functools

import jax
import jax.numpy as jnp
from jax import lax
from jax.experimental import pallas as pl
from jax.experimental.pallas import tpu as pltpu
from jax.sharding import PartitionSpec as P


TIME_STEP = 0.01
CUT_SQ = 6.25
SHIFT_FORCE = 24.0 * (2.0 * 2.5 ** (-13) - 2.5 ** (-7))
SPACING = 1.2
CELL_XY = 4.8
CELL_Z = 9.6
CELLS = 64
ATOMS = 128
F32 = jnp.float32
VMEM = pl.BlockSpec(memory_space=pltpu.VMEM)
SMEM = pl.BlockSpec(memory_space=pltpu.SMEM)


def lanes():
    return lax.broadcasted_iota(jnp.int32, (8, ATOMS), 1)


def rows8():
    return lax.broadcasted_iota(jnp.int32, (8, ATOMS), 0)


def low_half():
    return lanes() < CELLS


def swap_halves(v):
    return pltpu.roll(v, CELLS, 1)


def from_cell_below(v):
    at_edge = (lanes() & (CELLS - 1)) == 0
    return jnp.where(at_edge, pltpu.roll(v, CELLS + 1, 1), pltpu.roll(v, 1, 1))


def from_cell_above(v):
    at_edge = (lanes() & (CELLS - 1)) == CELLS - 1
    return jnp.where(at_edge, pltpu.roll(v, CELLS - 1, 1), pltpu.roll(v, ATOMS - 1, 1))


def lookup(values, index):
    return jnp.take_along_axis(values, index, axis=1)


def wrapped(step, count):
    step = jnp.where(step < 0, step + count, step)
    return jnp.where(step >= count, step - count, step)


def prepare_kernel(row_count, col_count, pos, vel, frc, tiles, counts,
                   moved_out, half_out, code_out, own_out, mask_out, pay_a, pay_b):
    my_row = lax.axis_index("row")
    my_col = lax.axis_index("col")

    half = vel[...] + (0.5 * TIME_STEP) * frc[...]
    moved = pos[...] + TIME_STEP * half
    half_out[...] = half
    moved_out[...] = moved

    place = pos[...]
    lowest = jnp.min(place, axis=2, keepdims=True)
    site = ((place - lowest) * (1.0 / SPACING) + 0.5).astype(jnp.int32)
    code = (site[1] >> 1) * 64 + site[0] * 16 + (site[1] & 1) * 8 + site[2]
    code_out[...] = code

    point = lax.broadcasted_iota(jnp.int32, (ATOMS, ATOMS), 0)
    spot = lax.broadcasted_iota(jnp.int32, (8, 8 * ATOMS), 1)
    line = lax.broadcasted_iota(jnp.int32, (8, 8 * ATOMS), 0)
    numbers = jnp.where(spot // ATOMS == line, spot % ATOMS, 0).astype(F32).astype(jnp.bfloat16)
    sorted_rows = [[], [], []]
    for group in range(CELLS // 8):
        hot = []
        for b in range(8):
            row = code[group * 8 + b : group * 8 + b + 1, :]
            hot.append(jnp.where(point == row, 1.0, 0.0).astype(jnp.bfloat16))
        hot = jnp.concatenate(hot, axis=1)
        atom = lax.dot_general(numbers, hot, (((1,), (1,)), ((), ())), preferred_element_type=F32)
        atom = atom.astype(jnp.int32)
        for k in range(3):
            sorted_rows[k].append(lookup(moved[k, group * 8 : group * 8 + 8, :], atom))

    own = []
    for k in range(3):
        cells_first = jnp.concatenate(sorted_rows[k], axis=0)
        both = jnp.concatenate([cells_first, pltpu.roll(cells_first, CELLS, 1)], axis=0)
        own.append(jnp.swapaxes(both, 0, 1)[:CELLS].reshape(4, 2, 8, ATOMS))
        own_out[k] = own[k]

    left = tiles[0:1, :]
    right = tiles[1:2, :]
    used = counts[0, 0]
    dx = 2 - wrapped(my_row - (right >> 6) + 1, row_count)
    dy = 2 - wrapped((left >> 6) - my_col + 1, col_count)
    dz = 2 - (((left & 63) - (right & 63) + 1) & 63)
    alive = lax.broadcasted_iota(jnp.int32, left.shape, 1) < used
    kind = jnp.where(alive, dy * 16 + dz * 3 + dx, -1)
    slots = left.shape[1]
    kind_hot = lax.broadcasted_iota(jnp.int32, (48, slots), 0) == kind
    cell_hot = (lax.broadcasted_iota(jnp.int32, (ATOMS, slots), 0) & 63) == (right & 63)
    mask = lax.dot_general(
        jnp.where(kind_hot, 1.0, 0.0).astype(jnp.bfloat16),
        jnp.where(cell_hot, 1.0, 0.0).astype(jnp.bfloat16),
        (((1,), (1,)), ((), ())), preferred_element_type=F32,
    ).reshape(3, 2, 8, ATOMS)
    mask_out[...] = mask[1]

    def pack(to_upper, to_lower):
        lo = low_half()
        for k in range(3):
            for x in range(4):
                first, second = own[k][x, 0], own[k][x, 1]
                up = jnp.where(lo, swap_halves(first), second)
                down = jnp.where(lo, first, swap_halves(second))
                if k == 1:
                    up = up - CELL_XY
                    down = down + CELL_XY
                to_upper[k * 4 + x] = up
                to_lower[k * 4 + x] = down
        to_upper[12:14] = mask[0]
        to_lower[12:14] = mask[2]

    odd = (my_col & 1) == 1

    @pl.when(odd)
    def _():
        pack(pay_a, pay_b)

    @pl.when(jnp.logical_not(odd))
    def _():
        pack(pay_b, pay_a)


def row_frames(own, frames):
    for k in range(3):
        for x in range(4):
            for yy in range(2):
                v = own[k, x, yy]
                below = from_cell_below(v)
                above = from_cell_above(v)
                if k == 2:
                    below = below - CELL_Z
                    above = above + CELL_Z
                for kz in (-2, -1, 0, 1, 2):
                    if kz == 0:
                        out = v
                    elif kz > 0:
                        out = pltpu.roll(jnp.where(rows8() >= 8 - kz, below, v), kz, 0)
                    else:
                        out = pltpu.roll(jnp.where(rows8() < -kz, above, v), 8 + kz, 0)
                    frames[kz + 2, k, x, yy] = out


def limits(mask_low, mask_own, mask_high, kz, dx, group):
    def row(mask, dz):
        index = (dz + 1) * 3 + dx + 1
        return jnp.broadcast_to(mask[index // 8, index % 8 : index % 8 + 1, :], (8, ATOMS))

    def both(dz):
        if group == 0:
            return jnp.where(low_half(), row(mask_low, dz), row(mask_own, dz))
        if group == 2:
            return jnp.where(low_half(), row(mask_own, dz), row(mask_high, dz))
        return row(mask_own, dz)

    inner = both(0)
    if kz > 0:
        inner = jnp.where(rows8() < kz, both(1), inner)
    if kz < 0:
        inner = jnp.where(rows8() >= 8 + kz, both(-1), inner)
    return inner * CUT_SQ


def spread(first, second, lower, upper):
    lo = low_half()
    return [
        jnp.where(lo, lower, swap_halves(first)),
        swap_halves(jnp.where(lo, second, lower)),
        first,
        second,
        swap_halves(jnp.where(lo, upper, first)),
        jnp.where(lo, swap_halves(second), upper),
    ]


def add_pairs(frames, before, total, partner, limit, columns, rows):
    for kz in (-2, -1, 0, 1, 2):
        for x in range(4):
            for yy in range(2):
                mine = [frames[kz + 2, k, x, yy] for k in range(3)]
                acc = [None if before is None else before[kz + 2, k, x, yy] for k in range(3)]
                for kx in (-2, -1, 0, 1, 2):
                    for ky in (-2, -1, 0, 1, 2):
                        if (abs(kx) == 2) + (abs(ky) == 2) + (abs(kz) == 2) > 1:
                            continue
                        if kx == 0 and ky == 0 and kz == 0:
                            continue
                        if x + kx not in columns or yy + ky + 2 not in rows:
                            continue
                        m = yy + ky + 2
                        away = [mine[k] - partner(k, x + kx, m) for k in range(3)]
                        dist = away[0] * away[0] + away[1] * away[1] + away[2] * away[2]
                        inside = (dist < limit(kz, (x + kx) // 4, m // 2)) & (dist > 0.25)
                        inv = lax.rsqrt(dist)
                        inv_sq = inv * inv
                        inv_six = inv_sq * inv_sq * inv_sq
                        weight = inv_sq * (inv_six * (48.0 * inv_six - 24.0)) - SHIFT_FORCE * inv
                        weight = jnp.where(inside, weight, 0.0)
                        for k in range(3):
                            term = weight * away[k]
                            acc[k] = term if acc[k] is None else acc[k] + term
                for k in range(3):
                    total[kz + 2, k, x, yy] = jnp.zeros((8, ATOMS), F32) if acc[k] is None else acc[k]


def own_kernel(own, mask, frames, total):
    row_frames(own, frames)
    table = {kz: limits(None, mask, None, kz, 0, 1) for kz in (-2, -1, 0, 1, 2)}
    add_pairs(frames, None, total, lambda k, x, m: own[k, x, m - 2], lambda kz, dx, g: table[kz],
              (0, 1, 2, 3), (2, 3))


def relay_kernel(own, got_a, got_b, pay_a, pay_b):
    col_odd = (lax.axis_index("col") & 1) == 1
    row_odd = (lax.axis_index("row") & 1) == 1

    def pack(ref, columns, offset):
        for k in range(3):
            for n, x in enumerate(columns):
                from_a, from_b = got_a[k * 4 + x], got_b[k * 4 + x]
                parts = [own[k, x, 0], own[k, x, 1],
                         jnp.where(col_odd, from_b, from_a), jnp.where(col_odd, from_a, from_b)]
                for i in range(4):
                    ref[k, n, i] = parts[i] + offset if k == 0 else parts[i]

    @pl.when(row_odd)
    def _():
        pack(pay_a, (2, 3), -CELL_XY)
        pack(pay_b, (0, 1), CELL_XY)

    @pl.when(jnp.logical_not(row_odd))
    def _():
        pack(pay_b, (2, 3), -CELL_XY)
        pack(pay_a, (0, 1), CELL_XY)


def column_kernel(own, mask, got_a, got_b, frames, total_in, total, table, near, outer):
    col_odd = (lax.axis_index("col") & 1) == 1
    for k in range(3):
        for x in range(4):
            from_a, from_b = got_a[k * 4 + x], got_b[k * 4 + x]
            lower = jnp.where(col_odd, from_b, from_a)
            upper = jnp.where(col_odd, from_a, from_b)
            six = spread(own[k, x, 0], own[k, x, 1], lower, upper)
            near[k, x, 0] = six[0]
            near[k, x, 1] = six[1]
            near[k, x, 2] = six[4]
            near[k, x, 3] = six[5]
    mask_a, mask_b = got_a[12:14], got_b[12:14]
    mask_low = jnp.where(col_odd, mask_b, mask_a)
    mask_high = jnp.where(col_odd, mask_a, mask_b)
    mask_own = mask[...]
    for kz in (-2, -1, 0, 1, 2):
        for g in range(3):
            for n, dx in enumerate((-1, 1)):
                table[kz + 2, n, g] = limits(mask_low, mask_own, mask_high, kz, dx, g)
            if g != 1:
                outer[kz + 2, g // 2] = limits(mask_low, mask_own, mask_high, kz, 0, g)
    add_pairs(frames, total_in, total, lambda k, x, m: near[k, x, m if m < 2 else m - 2],
              lambda kz, dx, g: outer[kz + 2, g // 2], (0, 1, 2, 3), (0, 1, 4, 5))


def finish_kernel(got_a, got_b, frames, total_in, table, half, code, new_vel, new_frc, total, side):
    row_odd = (lax.axis_index("row") & 1) == 1
    for k in range(3):
        for n in range(2):
            for s in range(2):
                parts = [jnp.where(row_odd == (s == 0), got_b[k, n, i], got_a[k, n, i]) for i in range(4)]
                six = spread(*parts)
                for m in range(6):
                    side[s, k, n, m] = six[m]

    def partner(k, x, m):
        return side[0, k, x + 2, m] if x < 0 else side[1, k, x - 4, m]

    add_pairs(frames, total_in, total, partner, lambda kz, dx, g: table[kz + 2, 0 if dx < 0 else 1, g],
              (-2, -1, 4, 5), (0, 1, 2, 3, 4, 5))

    row = rows8()
    lo = low_half()[0:1]
    for k in range(3):
        stacked = []
        for x in range(4):
            for yy in range(2):
                one_up = pltpu.roll(total[3, k, x, yy], 7, 0)
                two_up = pltpu.roll(total[4, k, x, yy], 6, 0)
                one_down = pltpu.roll(total[1, k, x, yy], 1, 0)
                two_down = pltpu.roll(total[0, k, x, yy], 2, 0)
                inner = total[2, k, x, yy] + jnp.where(row < 7, one_up, 0.0) + jnp.where(row < 6, two_up, 0.0)
                inner = inner + jnp.where(row > 0, one_down, 0.0) + jnp.where(row > 1, two_down, 0.0)
                above = jnp.where(row < 7, 0.0, one_up) + jnp.where(row < 6, 0.0, two_up)
                below = jnp.where(row > 0, 0.0, one_down) + jnp.where(row > 1, 0.0, two_down)
                stacked.append(inner + from_cell_above(above) + from_cell_below(below))
        lattice = jnp.concatenate(stacked, axis=0)
        flipped = jnp.swapaxes(jnp.concatenate([lattice, lattice], axis=0), 0, 1)
        cells_first = jnp.where(lo, flipped[:CELLS], flipped[CELLS:])
        for g in range(8):
            rows = slice(g * 8, g * 8 + 8)
            value = lookup(cells_first[rows], code[rows, :])
            new_frc[k, rows, :] = value
            new_vel[k, rows, :] = half[k, rows, :] + (0.5 * TIME_STEP) * value


def kernel_call(body, outs, args, specs=None, scratch=(), flops=0, name=None):
    moved = sum(4 * a.size for a in args) + sum(4 * s.size for s in outs)
    return pl.pallas_call(
        body,
        out_shape=outs,
        in_specs=[VMEM] * len(args) if specs is None else specs,
        out_specs=[VMEM] * len(outs),
        scratch_shapes=list(scratch),
        compiler_params=pltpu.CompilerParams(vmem_limit_bytes=8 << 20),
        cost_estimate=pl.CostEstimate(flops=flops, bytes_accessed=moved, transcendentals=0),
        name=name,
    )(*args)


def pairing(count, odd):
    if odd:
        return [(i, (i + 1) % count if i % 2 else (i - 1) % count) for i in range(count)]
    return [(i, i ^ 1) for i in range(count)]


def exchange(first, second, axis):
    count = lax.axis_size(axis)
    return (lax.ppermute(first, axis, pairing(count, True)), lax.ppermute(second, axis, pairing(count, False)))


def per_device(positions, velocities, forces, tiles, counts):
    blocks, _, atoms = positions.shape
    assert blocks == CELLS and atoms == ATOMS
    row_count, col_count = lax.axis_size("row"), lax.axis_size("col")
    assert row_count % 2 == 0 and col_count % 2 == 0 and min(row_count, col_count) > 2
    by_component = [jnp.transpose(a, (1, 0, 2)) for a in (positions, velocities, forces)]
    tile_rows = jnp.transpose(tiles[0, 0], (1, 0))

    def f32(*shape):
        return jax.ShapeDtypeStruct(shape, F32)

    span = f32(3, CELLS, ATOMS)
    lattice = f32(3, 4, 2, 8, ATOMS)
    moved, half, code, own, mask, pay_a, pay_b = kernel_call(
        functools.partial(prepare_kernel, row_count, col_count),
        [span, span, jax.ShapeDtypeStruct((CELLS, ATOMS), jnp.int32), lattice, f32(2, 8, ATOMS),
         f32(14, 8, ATOMS), f32(14, 8, ATOMS)],
        [*by_component, tile_rows, counts],
        specs=[VMEM, VMEM, VMEM, VMEM, SMEM], name="prepare",
    )
    got_a, got_b = exchange(pay_a, pay_b, "col")
    frames, total = kernel_call(own_kernel, [f32(5, 3, 4, 2, 8, ATOMS)] * 2, [own, mask], flops=10**8, name="own")
    side_a, side_b = kernel_call(relay_kernel, [f32(3, 2, 4, 8, ATOMS)] * 2, [own, got_a, got_b], name="relay")
    far_a, far_b = exchange(side_a, side_b, "row")
    total, table = kernel_call(
        column_kernel, [f32(5, 3, 4, 2, 8, ATOMS), f32(5, 2, 3, 8, ATOMS)],
        [own, mask, got_a, got_b, frames, total], flops=10**8, name="column",
        scratch=[pltpu.VMEM((3, 4, 4, 8, ATOMS), F32), pltpu.VMEM((5, 2, 8, ATOMS), F32)],
    )
    new_vel, new_frc = kernel_call(
        finish_kernel, [span, span], [far_a, far_b, frames, total, table, half, code], flops=10**8, name="finish",
        scratch=[pltpu.VMEM((5, 3, 4, 2, 8, ATOMS), F32), pltpu.VMEM((2, 3, 2, 6, 8, ATOMS), F32)],
    )
    return tuple(jnp.transpose(a, (1, 0, 2)) for a in (moved, new_vel, new_frc))


def solution(mesh):
    in_specs = (
        P(("row", "col"), None, None),
        P(("row", "col"), None, None),
        P(("row", "col"), None, None),
        P("row", "col", None, None),
        P("row", "col"),
    )
    out_specs = (
        P(("row", "col"), None, None),
        P(("row", "col"), None, None),
        P(("row", "col"), None, None),
    )
    return jax.shard_map(
        per_device, mesh=mesh, in_specs=in_specs, out_specs=out_specs, check_vma=False
    )
```

```python
import functools

import jax
import jax.numpy as jnp
from jax import lax
from jax.experimental import pallas as pl
from jax.experimental.pallas import tpu as pltpu
from jax.sharding import PartitionSpec as P


TIME_STEP = 0.01
CUT_SQ = 6.25
SHIFT_FORCE = 24.0 * (2.0 * 2.5 ** (-13) - 2.5 ** (-7))
SPACING = 1.2
CELL_XY = 4.8
CELL_Z = 9.6
CELLS = 64
ATOMS = 128
F32 = jnp.float32
VMEM = pl.BlockSpec(memory_space=pltpu.VMEM)
SMEM = pl.BlockSpec(memory_space=pltpu.SMEM)
HBM = pl.BlockSpec(memory_space=pltpu.HBM)


def lanes():
    return lax.broadcasted_iota(jnp.int32, (8, ATOMS), 1)


def rows8():
    return lax.broadcasted_iota(jnp.int32, (8, ATOMS), 0)


def low_half():
    return lanes() < CELLS


def swap_halves(v):
    return pltpu.roll(v, CELLS, 1)


def from_cell_below(v):
    at_edge = (lanes() & (CELLS - 1)) == 0
    return jnp.where(at_edge, pltpu.roll(v, CELLS + 1, 1), pltpu.roll(v, 1, 1))


def from_cell_above(v):
    at_edge = (lanes() & (CELLS - 1)) == CELLS - 1
    return jnp.where(at_edge, pltpu.roll(v, CELLS - 1, 1), pltpu.roll(v, ATOMS - 1, 1))


def lookup(values, index):
    return jnp.take_along_axis(values, index, axis=1)


def wrapped(step, count):
    step = jnp.where(step < 0, step + count, step)
    return jnp.where(step >= count, step - count, step)


def by_parity(index, pack, first, second):
    odd = (index & 1) == 1

    @pl.when(odd)
    def _():
        pack(first, second)

    @pl.when(jnp.logical_not(odd))
    def _():
        pack(second, first)


def prepare_kernel(row_count, col_count, pos_hbm, vel_hbm, frc_hbm, tiles_hbm, counts,
                   moved_out, half_out, code_out, own_out, mask_out, pay_a, pay_b, face_a, face_b,
                   pos, vel, frc, tiles, sems):
    my_row = lax.axis_index("row")
    my_col = lax.axis_index("col")
    copies = [pltpu.make_async_copy(tiles_hbm, tiles, sems.at[9])]
    for i, (source, target) in enumerate([(pos_hbm, pos), (vel_hbm, vel), (frc_hbm, frc)]):
        for k in range(3):
            copies.append(pltpu.make_async_copy(source.at[k], target.at[k], sems.at[i * 3 + k]))
    for copy in copies[1:4] + copies[:1] + copies[4:]:
        copy.start()
    for copy in copies[1:4]:
        copy.wait()

    place = pos[...]
    lowest = jnp.min(place, axis=2, keepdims=True)
    site = ((place - lowest) * (1.0 / SPACING) + 0.5).astype(jnp.int32)
    code = (site[1] >> 1) * 64 + site[0] * 16 + (site[1] & 1) * 8 + site[2]
    code_out[...] = code

    high, low = code >> 4, code & 15
    number = lax.broadcasted_iota(jnp.int32, (8, ATOMS), 1)
    digit = lax.broadcasted_iota(jnp.int32, (16, ATOMS), 0)
    pick = rows8() * 16 + (lanes() & 15)
    order = []
    for g in range(CELLS // 8):
        rows = slice(g * 8, g * 8 + 8)
        left = [jnp.where(high[rows] == h, number, 0).astype(F32) for h in range(8)]
        right = [jnp.where(digit == low[b : b + 1], 1.0, 0.0).astype(F32) for b in range(g * 8, g * 8 + 8)]
        found = lax.dot_general(
            jnp.concatenate(left, axis=0).astype(jnp.bfloat16), jnp.concatenate(right, axis=0).astype(jnp.bfloat16),
            (((1,), (1,)), ((), ())), preferred_element_type=F32,
        ).astype(jnp.int32)
        atom = lookup(found[:8], pick)
        for h in range(1, 8):
            atom = jnp.where(lanes() >= h * 16, lookup(found[h * 8 : h * 8 + 8], pick), atom)
        order.append(atom)

    for copy in copies[:1] + copies[4:]:
        copy.wait()
    half = vel[...] + (0.5 * TIME_STEP) * frc[...]
    moved = pos[...] + TIME_STEP * half
    half_out[...] = half
    moved_out[...] = moved

    own = []
    for k in range(3):
        cells_first = jnp.concatenate(
            [lookup(moved[k, g * 8 : g * 8 + 8, :], order[g]) for g in range(CELLS // 8)], axis=0
        )
        both = jnp.concatenate([cells_first, pltpu.roll(cells_first, CELLS, 1)], axis=0)
        own.append(jnp.swapaxes(both, 0, 1)[:CELLS].reshape(4, 2, 8, ATOMS))
        own_out[k] = own[k]

    left = tiles[0:1, :]
    right = tiles[1:2, :]
    used = counts[0, 0]
    dx = 2 - wrapped(my_row - (right >> 6) + 1, row_count)
    dy = 2 - wrapped((left >> 6) - my_col + 1, col_count)
    dz = 2 - (((left & 63) - (right & 63) + 1) & 63)
    alive = lax.broadcasted_iota(jnp.int32, left.shape, 1) < used
    kind = jnp.where(alive, dy * 16 + dz * 3 + dx, -1)
    slots = left.shape[1]
    kind_hot = lax.broadcasted_iota(jnp.int32, (48, slots), 0) == kind
    cell_hot = (lax.broadcasted_iota(jnp.int32, (ATOMS, slots), 0) & 63) == (right & 63)
    mask = lax.dot_general(
        jnp.where(kind_hot, 1.0, 0.0).astype(jnp.bfloat16),
        jnp.where(cell_hot, 1.0, 0.0).astype(jnp.bfloat16),
        (((1,), (1,)), ((), ())), preferred_element_type=F32,
    ).reshape(3, 2, 8, ATOMS)
    mask_out[...] = mask[1]

    def pack(to_upper, to_lower):
        lo = low_half()
        for k in range(3):
            for x in range(4):
                first, second = own[k][x, 0], own[k][x, 1]
                up = jnp.where(lo, swap_halves(first), second)
                down = jnp.where(lo, first, swap_halves(second))
                if k == 1:
                    up = up - CELL_XY
                    down = down + CELL_XY
                to_upper[k * 4 + x] = up
                to_lower[k * 4 + x] = down
        to_upper[12:14] = mask[0]
        to_lower[12:14] = mask[2]

    def pack_faces(to_upper, to_lower):
        for k in range(3):
            for yy in range(2):
                for n in range(2):
                    up, down = own[k][2 + n, yy], own[k][n, yy]
                    to_upper[k, n, yy] = up - CELL_XY if k == 0 else up
                    to_lower[k, n, yy] = down + CELL_XY if k == 0 else down

    by_parity(my_col, pack, pay_a, pay_b)
    by_parity(my_row, pack_faces, face_a, face_b)


def row_frames(own, frames):
    for k in range(3):
        for x in range(4):
            for yy in range(2):
                v = own[k, x, yy]
                below = from_cell_below(v)
                above = from_cell_above(v)
                if k == 2:
                    below = below - CELL_Z
                    above = above + CELL_Z
                for kz in (-2, -1, 0, 1, 2):
                    if kz == 0:
                        out = v
                    elif kz > 0:
                        out = pltpu.roll(jnp.where(rows8() >= 8 - kz, below, v), kz, 0)
                    else:
                        out = pltpu.roll(jnp.where(rows8() < -kz, above, v), 8 + kz, 0)
                    frames[kz + 2, k, x, yy] = out


def limits(mask_low, mask_own, mask_high, kz, dx, group):
    def row(mask, dz):
        index = (dz + 1) * 3 + dx + 1
        return jnp.broadcast_to(mask[index // 8, index % 8 : index % 8 + 1, :], (8, ATOMS))

    def both(dz):
        if group == 0:
            return jnp.where(low_half(), row(mask_low, dz), row(mask_own, dz))
        if group == 2:
            return jnp.where(low_half(), row(mask_own, dz), row(mask_high, dz))
        if group == 3:
            return jnp.where(low_half(), row(mask_low, dz), row(mask_high, dz))
        return row(mask_own, dz)

    inner = both(0)
    if kz > 0:
        inner = jnp.where(rows8() < kz, both(1), inner)
    if kz < 0:
        inner = jnp.where(rows8() >= 8 + kz, both(-1), inner)
    return inner * CUT_SQ


def spread(first, second, lower, upper):
    lo = low_half()
    return [
        jnp.where(lo, lower, swap_halves(first)),
        swap_halves(jnp.where(lo, second, lower)),
        first,
        second,
        swap_halves(jnp.where(lo, upper, first)),
        jnp.where(lo, swap_halves(second), upper),
    ]


def add_pair(acc, mine, theirs, limit):
    away = [mine[k] - theirs[k] for k in range(3)]
    dist = away[0] * away[0] + away[1] * away[1] + away[2] * away[2]
    inside = (dist < limit) & (dist > 0.25)
    inv = lax.rsqrt(dist)
    inv_sq = inv * inv
    inv_six = inv_sq * inv_sq * inv_sq
    weight = inv_sq * (inv_six * (48.0 * inv_six - 24.0)) - SHIFT_FORCE * inv
    weight = jnp.where(inside, weight, 0.0)
    for k in range(3):
        term = weight * away[k]
        acc[k] = term if acc[k] is None else acc[k] + term


def in_range(*steps):
    return sum(abs(step) == 2 for step in steps) < 2


def row_frame(parts):
    row = rows8()
    total, above, below = parts.get(0), None, None
    for kz, part in parts.items():
        if kz == 0:
            continue
        back = pltpu.roll(part, (8 - kz) % 8, 0)
        stays = row < 8 - kz if kz > 0 else row >= -kz
        kept, passed = jnp.where(stays, back, 0.0), jnp.where(stays, 0.0, back)
        total = kept if total is None else total + kept
        if kz > 0:
            above = passed if above is None else above + passed
        else:
            below = passed if below is None else below + passed
    if above is not None:
        total = total + from_cell_above(above)
    if below is not None:
        total = total + from_cell_below(below)
    return total


def add_pairs(frames, before, total, partner, limit, columns, rows):
    for kz in (-2, -1, 0, 1, 2):
        for x in range(4):
            for yy in range(2):
                mine = [frames[kz + 2, k, x, yy] for k in range(3)]
                acc = [None if before is None else before[kz + 2, k, x, yy] for k in range(3)]
                for kx in (-2, -1, 0, 1, 2):
                    for ky in (-2, -1, 0, 1, 2):
                        if not in_range(kx, ky, kz):
                            continue
                        if kx == 0 and ky == 0 and kz == 0:
                            continue
                        if x + kx not in columns or yy + ky + 2 not in rows:
                            continue
                        m = yy + ky + 2
                        add_pair(acc, mine, [partner(k, x + kx, m) for k in range(3)],
                                 limit(kz, (x + kx) // 4, m // 2))
                for k in range(3):
                    total[kz + 2, k, x, yy] = jnp.zeros((8, ATOMS), F32) if acc[k] is None else acc[k]


def own_kernel(own, mask, moved, frames, total, moved_out, sem):
    leaving = pltpu.make_async_copy(moved, moved_out, sem)
    leaving.start()
    row_frames(own, frames)
    table = {kz: limits(None, mask, None, kz, 0, 1) for kz in (-2, -1, 0, 1, 2)}
    add_pairs(frames, None, total, lambda k, x, m: own[k, x, m - 2], lambda kz, dx, g: table[kz],
              (0, 1, 2, 3), (2, 3))
    leaving.wait()


def relay_kernel(got_a, got_b, pay_a, pay_b):
    col_odd = (lax.axis_index("col") & 1) == 1
    lo = low_half()

    def pack(ref, near, far, offset):
        for k in range(3):
            for x in (near, far):
                from_a, from_b = got_a[k * 4 + x], got_b[k * 4 + x]
                if k == 0:
                    from_a, from_b = from_a + offset, from_b + offset
                lower = jnp.where(col_odd, from_b, from_a)
                upper = jnp.where(col_odd, from_a, from_b)
                ref[k, 0 if x == near else 2] = swap_halves(jnp.where(lo, upper, lower))
                if x == near:
                    ref[k, 1] = jnp.where(lo, lower, upper)

    def both(to_upper, to_lower):
        pack(to_upper, 3, 2, -CELL_XY)
        pack(to_lower, 0, 1, CELL_XY)

    by_parity(lax.axis_index("row"), both, pay_a, pay_b)


def column_kernel(own, mask, got_a, got_b, frames, total_in, total, table, near, outer):
    col_odd = (lax.axis_index("col") & 1) == 1
    for k in range(3):
        for x in range(4):
            from_a, from_b = got_a[k * 4 + x], got_b[k * 4 + x]
            lower = jnp.where(col_odd, from_b, from_a)
            upper = jnp.where(col_odd, from_a, from_b)
            six = spread(own[k, x, 0], own[k, x, 1], lower, upper)
            near[k, x, 0] = six[0]
            near[k, x, 1] = six[1]
            near[k, x, 2] = six[4]
            near[k, x, 3] = six[5]
    mask_a, mask_b = got_a[12:14], got_b[12:14]
    mask_low = jnp.where(col_odd, mask_b, mask_a)
    mask_high = jnp.where(col_odd, mask_a, mask_b)
    mask_own = mask[...]
    for kz in (-2, -1, 0, 1, 2):
        for n, dx in enumerate((-1, 1)):
            table[kz + 2, n, 0] = limits(mask_low, mask_own, mask_high, kz, dx, 1)
            table[kz + 2, n, 1] = limits(mask_low, mask_own, mask_high, kz, dx, 3)
        for g in (0, 2):
            outer[kz + 2, g // 2] = limits(mask_low, mask_own, mask_high, kz, 0, g)
    add_pairs(frames, total_in, total, lambda k, x, m: near[k, x, m if m < 2 else m - 2],
              lambda kz, dx, g: outer[kz + 2, g // 2], (0, 1, 2, 3), (0, 1, 4, 5))


def row_kernel(face_a, face_b, frames, total_in, table, base, side):
    row_odd = (lax.axis_index("row") & 1) == 1
    lo = low_half()
    for k in range(3):
        for n in range(2):
            first, second = face_a[k, n], face_b[k, n]
            for s in range(2):
                zero, one = [jnp.where(row_odd == (s == 0), second[yy], first[yy]) for yy in range(2)]
                side[s, k, n, 0] = zero
                side[s, k, n, 1] = one
                side[s, k, n, 2] = swap_halves(zero)
                side[s, k, n, 3] = swap_halves(one)
                side[s, k, n, 4] = swap_halves(jnp.where(lo, one, zero))

    for x in range(4):
        parts = [[{} for _ in range(3)] for _ in range(3)]
        for kz in (-2, -1, 0, 1, 2):
            mine = [[frames[kz + 2, k, x, yy] for k in range(3)] for yy in range(2)]
            inner = [jnp.where(lo, mine[1][k], mine[0][k]) for k in range(3)]
            acc = [[total_in[kz + 2, k, x, yy] for k in range(3)] for yy in range(2)]
            cross = [None] * 3
            for kx in (-2, -1, 1, 2):
                if 0 <= x + kx < 4:
                    continue
                s, n = (0, x + kx + 2) if kx < 0 else (1, x + kx - 4)
                limit = table[kz + 2, s, 0]
                for yy in range(2):
                    for i, ky in ((0, -yy), (1, 1 - yy), (2 + yy, 2)):
                        if in_range(kx, ky, kz):
                            add_pair(acc[yy], mine[yy], [side[s, k, n, i] for k in range(3)], limit)
                if in_range(kx, 1, kz):
                    add_pair(cross, inner, [side[s, k, n, 4] for k in range(3)], limit)
            for k in range(3):
                parts[0][k][kz], parts[1][k][kz] = acc[0][k], acc[1][k]
                if cross[k] is not None:
                    parts[2][k][kz] = cross[k]
        for k in range(3):
            zero, one, cross = [row_frame(parts[i][k]) for i in range(3)]
            base[k, x, 0] = zero + jnp.where(lo, 0.0, cross)
            base[k, x, 1] = one + jnp.where(lo, cross, 0.0)


def finish_kernel(got_a, got_b, frames, base, table, half, code, vel_out, frc_out, corner, new_vel, new_frc, sems):
    row_odd = (lax.axis_index("row") & 1) == 1
    lo = low_half()
    for k in range(3):
        for s in range(2):
            for i in range(3):
                corner[s, k, i] = jnp.where(row_odd == (s == 0), got_b[k, i], got_a[k, i])

    added = [[None] * 4 for _ in range(3)]
    for x in range(4):
        s, step = (0, -1) if x < 2 else (1, 1)
        edge = x in (0, 3)
        outer_parts, inner_parts = [{} for _ in range(3)], [{} for _ in range(3)]
        for kz in (-2, -1, 0, 1, 2):
            if abs(kz) == 2 and not edge:
                continue
            limit = table[kz + 2, s, 1]
            mine = [[frames[kz + 2, k, x, yy] for k in range(3)] for yy in range(2)]
            outer = [jnp.where(lo, mine[0][k], mine[1][k]) for k in range(3)]
            inner = [jnp.where(lo, mine[1][k], mine[0][k]) for k in range(3)]
            near, far, deep = [[corner[s, k, i] for k in range(3)] for i in range(3)]
            on_outer, on_inner = [None] * 3, [None] * 3
            if edge:
                add_pair(on_outer, outer, near, limit)
                if in_range(1, 2, kz):
                    add_pair(on_outer, outer, far, limit)
                    add_pair(on_inner, inner, near, limit)
            if in_range(2, 1, kz):
                add_pair(on_outer, outer, deep if edge else near, limit)
            for k in range(3):
                outer_parts[k][kz] = on_outer[k]
                if on_inner[k] is not None:
                    inner_parts[k][kz] = on_inner[k]
        for k in range(3):
            on_outer = row_frame(outer_parts[k])
            on_inner = row_frame(inner_parts[k]) if edge else 0.0
            added[k][x] = (on_outer, on_inner)

    copies = []
    for k in range(3):
        stacked = []
        for x in range(4):
            on_outer, on_inner = added[k][x]
            stacked.append(base[k, x, 0] + jnp.where(lo, on_outer, on_inner))
            stacked.append(base[k, x, 1] + jnp.where(lo, on_inner, on_outer))
        lattice = jnp.concatenate(stacked, axis=0)
        flipped = jnp.swapaxes(jnp.concatenate([lattice, lattice], axis=0), 0, 1)
        cells_first = jnp.where(lo[0:1], flipped[:CELLS], flipped[CELLS:])
        for g in range(8):
            rows = slice(g * 8, g * 8 + 8)
            value = lookup(cells_first[rows], code[rows, :])
            new_frc[k, rows, :] = value
            new_vel[k, rows, :] = half[k, rows, :] + (0.5 * TIME_STEP) * value
        leaving = [pltpu.make_async_copy(new_frc.at[k], frc_out.at[k], sems.at[k]),
                   pltpu.make_async_copy(new_vel.at[k], vel_out.at[k], sems.at[3 + k])]
        for copy in leaving:
            copy.start()
        copies += leaving
    for copy in copies:
        copy.wait()


def kernel_call(body, outs, args, specs=None, outs_specs=None, scratch=(), flops=0, name=None):
    moved = sum(4 * a.size for a in args) + sum(4 * s.size for s in outs)
    return pl.pallas_call(
        body,
        out_shape=outs,
        in_specs=[VMEM] * len(args) if specs is None else specs,
        out_specs=[VMEM] * len(outs) if outs_specs is None else outs_specs,
        scratch_shapes=list(scratch),
        compiler_params=pltpu.CompilerParams(vmem_limit_bytes=8 << 20),
        cost_estimate=pl.CostEstimate(flops=flops, bytes_accessed=moved, transcendentals=0),
        name=name,
    )(*args)


def pairing(count, odd):
    if odd:
        return [(i, (i + 1) % count if i % 2 else (i - 1) % count) for i in range(count)]
    return [(i, i ^ 1) for i in range(count)]


def exchange(first, second, axis):
    count = lax.axis_size(axis)
    return (lax.ppermute(first, axis, pairing(count, True)), lax.ppermute(second, axis, pairing(count, False)))


def per_device(positions, velocities, forces, tiles, counts):
    blocks, _, atoms = positions.shape
    assert blocks == CELLS and atoms == ATOMS
    row_count, col_count = lax.axis_size("row"), lax.axis_size("col")
    assert row_count % 2 == 0 and col_count % 2 == 0 and min(row_count, col_count) > 2
    by_component = [jnp.transpose(a, (1, 0, 2)) for a in (positions, velocities, forces)]
    tile_rows = jnp.transpose(tiles[0, 0], (1, 0))

    def f32(*shape):
        return jax.ShapeDtypeStruct(shape, F32)

    span = f32(3, CELLS, ATOMS)
    lattice = f32(3, 4, 2, 8, ATOMS)
    sums = f32(5, 3, 4, 2, 8, ATOMS)
    moved, half, code, own, mask, pay_a, pay_b, face_a, face_b = kernel_call(
        functools.partial(prepare_kernel, row_count, col_count),
        [span, span, jax.ShapeDtypeStruct((CELLS, ATOMS), jnp.int32), lattice, f32(2, 8, ATOMS),
         f32(14, 8, ATOMS), f32(14, 8, ATOMS), f32(3, 2, 2, 8, ATOMS), f32(3, 2, 2, 8, ATOMS)],
        [*(pltpu.with_memory_space_constraint(a, pltpu.HBM) for a in (*by_component, tile_rows)), counts],
        specs=[HBM, HBM, HBM, HBM, SMEM], name="prepare",
        scratch=[pltpu.VMEM(span.shape, F32)] * 3
        + [pltpu.VMEM(tile_rows.shape, jnp.int32), pltpu.SemaphoreType.DMA((10,))],
    )
    got_a, got_b = exchange(pay_a, pay_b, "col")
    face_a, face_b = exchange(face_a, face_b, "row")
    frames, total, moved = kernel_call(own_kernel, [sums, sums, span], [own, mask, moved], flops=10**8, name="own",
                                       outs_specs=[VMEM, VMEM, HBM], scratch=[pltpu.SemaphoreType.DMA])
    far_a, far_b = exchange(
        *kernel_call(relay_kernel, [f32(3, 3, 8, ATOMS)] * 2, [got_a, got_b], name="relay"), "row"
    )
    total, table = kernel_call(
        column_kernel, [sums, f32(5, 2, 2, 8, ATOMS)],
        [own, mask, got_a, got_b, frames, total], flops=10**8, name="column",
        scratch=[pltpu.VMEM((3, 4, 4, 8, ATOMS), F32), pltpu.VMEM((5, 2, 8, ATOMS), F32)],
    )
    (base,) = kernel_call(
        row_kernel, [lattice], [face_a, face_b, frames, total, table], flops=10**8, name="rows",
        scratch=[pltpu.VMEM((2, 3, 2, 5, 8, ATOMS), F32)],
    )
    new_vel, new_frc = kernel_call(
        finish_kernel, [span, span], [far_a, far_b, frames, base, table, half, code], flops=10**8,
        name="finish", outs_specs=[HBM, HBM],
        scratch=[pltpu.VMEM((2, 3, 3, 8, ATOMS), F32), pltpu.VMEM(span.shape, F32), pltpu.VMEM(span.shape, F32),
                 pltpu.SemaphoreType.DMA((6,))],
    )
    return tuple(jnp.transpose(a, (1, 0, 2)) for a in (moved, new_vel, new_frc))


def solution(mesh):
    in_specs = (
        P(("row", "col"), None, None),
        P(("row", "col"), None, None),
        P(("row", "col"), None, None),
        P("row", "col", None, None),
        P("row", "col"),
    )
    out_specs = (
        P(("row", "col"), None, None),
        P(("row", "col"), None, None),
        P(("row", "col"), None, None),
    )
    return jax.shard_map(
        per_device, mesh=mesh, in_specs=in_specs, out_specs=out_specs, check_vma=False
    )
```

```python
import functools

import jax
import jax.numpy as jnp
from jax import lax
from jax.experimental import pallas as pl
from jax.experimental.pallas import tpu as pltpu
from jax.sharding import PartitionSpec as P


TIME_STEP = 0.01
CUT_SQ = 6.25
SHIFT_FORCE = 24.0 * (2.0 * 2.5 ** (-13) - 2.5 ** (-7))
SPACING = 1.2
CELL_XY = 4.8
CELL_Z = 9.6
CELLS = 64
ATOMS = 128
F32 = jnp.float32
VMEM = pl.BlockSpec(memory_space=pltpu.VMEM)
SMEM = pl.BlockSpec(memory_space=pltpu.SMEM)
HBM = pl.BlockSpec(memory_space=pltpu.HBM)


def lanes():
    return lax.broadcasted_iota(jnp.int32, (8, ATOMS), 1)


def rows8():
    return lax.broadcasted_iota(jnp.int32, (8, ATOMS), 0)


def low_half():
    return lanes() < CELLS


def swap_halves(v):
    return pltpu.roll(v, CELLS, 1)


def from_cell_below(v):
    at_edge = (lanes() & (CELLS - 1)) == 0
    return jnp.where(at_edge, pltpu.roll(v, CELLS + 1, 1), pltpu.roll(v, 1, 1))


def from_cell_above(v):
    at_edge = (lanes() & (CELLS - 1)) == CELLS - 1
    return jnp.where(at_edge, pltpu.roll(v, CELLS - 1, 1), pltpu.roll(v, ATOMS - 1, 1))


def lookup(values, index):
    return jnp.take_along_axis(values, index, axis=1)


def wrapped(step, count):
    step = jnp.where(step < 0, step + count, step)
    return jnp.where(step >= count, step - count, step)


def by_parity(index, pack, first, second):
    odd = (index & 1) == 1

    @pl.when(odd)
    def _():
        pack(first, second)

    @pl.when(jnp.logical_not(odd))
    def _():
        pack(second, first)


def prepare_kernel(row_count, col_count, pos_hbm, vel_hbm, frc_hbm, tiles_hbm, counts,
                   moved_out, half_out, code_out, own_out, mask_out, pay_a, pay_b, face_a, face_b,
                   pos, vel, frc, tiles, sems):
    my_row = lax.axis_index("row")
    my_col = lax.axis_index("col")
    copies = [pltpu.make_async_copy(tiles_hbm, tiles, sems.at[9])]
    for i, (source, target) in enumerate([(pos_hbm, pos), (vel_hbm, vel), (frc_hbm, frc)]):
        for k in range(3):
            copies.append(pltpu.make_async_copy(source.at[k], target.at[k], sems.at[i * 3 + k]))
    for copy in copies[1:4] + copies[:1] + copies[4:]:
        copy.start()
    for copy in copies[1:4]:
        copy.wait()

    place = pos[...]
    lowest = jnp.min(place, axis=2, keepdims=True)
    site = ((place - lowest) * (1.0 / SPACING) + 0.5).astype(jnp.int32)
    code = (site[1] >> 1) * 64 + site[0] * 16 + (site[1] & 1) * 8 + site[2]
    code_out[...] = code

    high, low = code >> 4, code & 15
    number = lax.broadcasted_iota(jnp.int32, (8, ATOMS), 1)
    digit = lax.broadcasted_iota(jnp.int32, (16, ATOMS), 0)
    pick = rows8() * 16 + (lanes() & 15)
    order = []
    for g in range(CELLS // 8):
        rows = slice(g * 8, g * 8 + 8)
        left = [jnp.where(high[rows] == h, number, 0).astype(F32) for h in range(8)]
        right = [jnp.where(digit == low[b : b + 1], 1.0, 0.0).astype(F32) for b in range(g * 8, g * 8 + 8)]
        found = lax.dot_general(
            jnp.concatenate(left, axis=0).astype(jnp.bfloat16), jnp.concatenate(right, axis=0).astype(jnp.bfloat16),
            (((1,), (1,)), ((), ())), preferred_element_type=F32,
        ).astype(jnp.int32)
        atom = lookup(found[:8], pick)
        for h in range(1, 8):
            atom = jnp.where(lanes() >= h * 16, lookup(found[h * 8 : h * 8 + 8], pick), atom)
        order.append(atom)

    for copy in copies[:1] + copies[4:]:
        copy.wait()
    half = vel[...] + (0.5 * TIME_STEP) * frc[...]
    moved = pos[...] + TIME_STEP * half
    half_out[...] = half
    moved_out[...] = moved

    own = []
    for k in range(3):
        cells_first = jnp.concatenate(
            [lookup(moved[k, g * 8 : g * 8 + 8, :], order[g]) for g in range(CELLS // 8)], axis=0
        )
        both = jnp.concatenate([cells_first, pltpu.roll(cells_first, CELLS, 1)], axis=0)
        own.append(jnp.swapaxes(both, 0, 1)[:CELLS].reshape(4, 2, 8, ATOMS))
        own_out[k] = own[k]

    left = tiles[0:1, :]
    right = tiles[1:2, :]
    used = counts[0, 0]
    dx = 2 - wrapped(my_row - (right >> 6) + 1, row_count)
    dy = 2 - wrapped((left >> 6) - my_col + 1, col_count)
    dz = 2 - (((left & 63) - (right & 63) + 1) & 63)
    alive = lax.broadcasted_iota(jnp.int32, left.shape, 1) < used
    kind = jnp.where(alive, dy * 16 + dz * 3 + dx, -1)
    slots = left.shape[1]
    kind_hot = lax.broadcasted_iota(jnp.int32, (48, slots), 0) == kind
    cell_hot = (lax.broadcasted_iota(jnp.int32, (ATOMS, slots), 0) & 63) == (right & 63)
    mask = lax.dot_general(
        jnp.where(kind_hot, 1.0, 0.0).astype(jnp.bfloat16),
        jnp.where(cell_hot, 1.0, 0.0).astype(jnp.bfloat16),
        (((1,), (1,)), ((), ())), preferred_element_type=F32,
    ).reshape(3, 2, 8, ATOMS)
    mask_out[...] = mask[1]

    def pack(to_upper, to_lower):
        lo = low_half()
        for k in range(3):
            for x in range(4):
                first, second = own[k][x, 0], own[k][x, 1]
                up = jnp.where(lo, swap_halves(first), second)
                down = jnp.where(lo, first, swap_halves(second))
                if k == 1:
                    up = up - CELL_XY
                    down = down + CELL_XY
                to_upper[k * 4 + x] = up
                to_lower[k * 4 + x] = down
        to_upper[12:14] = mask[0]
        to_lower[12:14] = mask[2]

    def pack_faces(to_upper, to_lower):
        for k in range(3):
            for yy in range(2):
                for n in range(2):
                    up, down = own[k][2 + n, yy], own[k][n, yy]
                    to_upper[k, n, yy] = up - CELL_XY if k == 0 else up
                    to_lower[k, n, yy] = down + CELL_XY if k == 0 else down

    by_parity(my_col, pack, pay_a, pay_b)
    pack_faces(face_a, face_b)


def row_frames(own, frames):
    for k in range(3):
        for x in range(4):
            for yy in range(2):
                v = own[k, x, yy]
                below = from_cell_below(v)
                above = from_cell_above(v)
                if k == 2:
                    below = below - CELL_Z
                    above = above + CELL_Z
                for kz in (-2, -1, 0, 1, 2):
                    if kz == 0:
                        out = v
                    elif kz > 0:
                        out = pltpu.roll(jnp.where(rows8() >= 8 - kz, below, v), kz, 0)
                    else:
                        out = pltpu.roll(jnp.where(rows8() < -kz, above, v), 8 + kz, 0)
                    frames[kz + 2, k, x, yy] = out


def limits(mask_low, mask_own, mask_high, kz, dx, group):
    def row(mask, dz):
        index = (dz + 1) * 3 + dx + 1
        return jnp.broadcast_to(mask[index // 8, index % 8 : index % 8 + 1, :], (8, ATOMS))

    def both(dz):
        if group == 0:
            return jnp.where(low_half(), row(mask_low, dz), row(mask_own, dz))
        if group == 2:
            return jnp.where(low_half(), row(mask_own, dz), row(mask_high, dz))
        if group == 3:
            return jnp.where(low_half(), row(mask_low, dz), row(mask_high, dz))
        return row(mask_own, dz)

    inner = both(0)
    if kz > 0:
        inner = jnp.where(rows8() < kz, both(1), inner)
    if kz < 0:
        inner = jnp.where(rows8() >= 8 + kz, both(-1), inner)
    return inner * CUT_SQ


def spread(first, second, lower, upper):
    lo = low_half()
    return [
        jnp.where(lo, lower, swap_halves(first)),
        swap_halves(jnp.where(lo, second, lower)),
        first,
        second,
        swap_halves(jnp.where(lo, upper, first)),
        jnp.where(lo, swap_halves(second), upper),
    ]


def add_pair(acc, mine, theirs, limit):
    away = [mine[k] - theirs[k] for k in range(3)]
    dist = away[0] * away[0] + away[1] * away[1] + away[2] * away[2]
    inside = (dist < limit) & (dist > 0.25)
    inv = lax.rsqrt(dist)
    inv_sq = inv * inv
    inv_six = inv_sq * inv_sq * inv_sq
    weight = inv_sq * (inv_six * (48.0 * inv_six - 24.0)) - SHIFT_FORCE * inv
    weight = jnp.where(inside, weight, 0.0)
    for k in range(3):
        term = weight * away[k]
        acc[k] = term if acc[k] is None else acc[k] + term


def in_range(*steps):
    return sum(abs(step) == 2 for step in steps) < 2


def row_frame(parts):
    row = rows8()
    total, above, below = parts.get(0), None, None
    for kz, part in parts.items():
        if kz == 0:
            continue
        back = pltpu.roll(part, (8 - kz) % 8, 0)
        stays = row < 8 - kz if kz > 0 else row >= -kz
        kept, passed = jnp.where(stays, back, 0.0), jnp.where(stays, 0.0, back)
        total = kept if total is None else total + kept
        if kz > 0:
            above = passed if above is None else above + passed
        else:
            below = passed if below is None else below + passed
    if above is not None:
        total = total + from_cell_above(above)
    if below is not None:
        total = total + from_cell_below(below)
    return total


def add_pairs(frames, before, total, partner, limit, columns, rows):
    for kz in (-2, -1, 0, 1, 2):
        for x in range(4):
            for yy in range(2):
                mine = [frames[kz + 2, k, x, yy] for k in range(3)]
                acc = [None if before is None else before[kz + 2, k, x, yy] for k in range(3)]
                for kx in (-2, -1, 0, 1, 2):
                    for ky in (-2, -1, 0, 1, 2):
                        if not in_range(kx, ky, kz):
                            continue
                        if kx == 0 and ky == 0 and kz == 0:
                            continue
                        if x + kx not in columns or yy + ky + 2 not in rows:
                            continue
                        m = yy + ky + 2
                        add_pair(acc, mine, [partner(k, x + kx, m) for k in range(3)],
                                 limit(kz, (x + kx) // 4, m // 2))
                for k in range(3):
                    total[kz + 2, k, x, yy] = jnp.zeros((8, ATOMS), F32) if acc[k] is None else acc[k]


def own_kernel(own, mask, moved, frames, total, moved_out, sem):
    leaving = pltpu.make_async_copy(moved, moved_out, sem)
    leaving.start()
    row_frames(own, frames)
    table = {kz: limits(None, mask, None, kz, 0, 1) for kz in (-2, -1, 0, 1, 2)}
    add_pairs(frames, None, total, lambda k, x, m: own[k, x, m - 2], lambda kz, dx, g: table[kz],
              (0, 1, 2, 3), (2, 3))
    leaving.wait()


def relay_kernel(got_a, got_b, pay_a, pay_b):
    col_odd = (lax.axis_index("col") & 1) == 1
    lo = low_half()

    def pack(ref, near, far, offset):
        for k in range(3):
            for x in (near, far):
                from_a, from_b = got_a[k * 4 + x], got_b[k * 4 + x]
                if k == 0:
                    from_a, from_b = from_a + offset, from_b + offset
                lower = jnp.where(col_odd, from_b, from_a)
                upper = jnp.where(col_odd, from_a, from_b)
                ref[k, 0 if x == near else 2] = jnp.where(lo, upper, lower)
                if x == near:
                    ref[k, 1] = jnp.where(lo, lower, upper)

    def both(to_upper, to_lower):
        pack(to_upper, 3, 2, -CELL_XY)
        pack(to_lower, 0, 1, CELL_XY)

    both(pay_a, pay_b)


def column_kernel(own, mask, got_a, got_b, frames, total_in, total, table, near, outer):
    col_odd = (lax.axis_index("col") & 1) == 1
    for k in range(3):
        for x in range(4):
            from_a, from_b = got_a[k * 4 + x], got_b[k * 4 + x]
            lower = jnp.where(col_odd, from_b, from_a)
            upper = jnp.where(col_odd, from_a, from_b)
            six = spread(own[k, x, 0], own[k, x, 1], lower, upper)
            near[k, x, 0] = six[0]
            near[k, x, 1] = six[1]
            near[k, x, 2] = six[4]
            near[k, x, 3] = six[5]
    mask_a, mask_b = got_a[12:14], got_b[12:14]
    mask_low = jnp.where(col_odd, mask_b, mask_a)
    mask_high = jnp.where(col_odd, mask_a, mask_b)
    mask_own = mask[...]
    for kz in (-2, -1, 0, 1, 2):
        for n, dx in enumerate((-1, 1)):
            table[kz + 2, n, 0] = limits(mask_low, mask_own, mask_high, kz, dx, 1)
            table[kz + 2, n, 1] = limits(mask_low, mask_own, mask_high, kz, dx, 3)
        for g in (0, 2):
            outer[kz + 2, g // 2] = limits(mask_low, mask_own, mask_high, kz, 0, g)
    add_pairs(frames, total_in, total, lambda k, x, m: near[k, x, m if m < 2 else m - 2],
              lambda kz, dx, g: outer[kz + 2, g // 2], (0, 1, 2, 3), (0, 1, 4, 5))


def row_kernel(face_a, face_b, frames, total_in, table, base, side):
    lo = low_half()
    for k in range(3):
        for n in range(2):
            first, second = face_a[k, n], face_b[k, n]
            for s in range(2):
                zero, one = [(second if s == 0 else first)[yy] for yy in range(2)]
                side[s, k, n, 0] = zero
                side[s, k, n, 1] = one
                side[s, k, n, 2] = swap_halves(zero)
                side[s, k, n, 3] = swap_halves(one)
                side[s, k, n, 4] = swap_halves(jnp.where(lo, one, zero))

    for x in range(4):
        parts = [[{} for _ in range(3)] for _ in range(3)]
        for kz in (-2, -1, 0, 1, 2):
            mine = [[frames[kz + 2, k, x, yy] for k in range(3)] for yy in range(2)]
            inner = [jnp.where(lo, mine[1][k], mine[0][k]) for k in range(3)]
            acc = [[total_in[kz + 2, k, x, yy] for k in range(3)] for yy in range(2)]
            cross = [None] * 3
            for kx in (-2, -1, 1, 2):
                if 0 <= x + kx < 4:
                    continue
                s, n = (0, x + kx + 2) if kx < 0 else (1, x + kx - 4)
                limit = table[kz + 2, s, 0]
                for yy in range(2):
                    for i, ky in ((0, -yy), (1, 1 - yy), (2 + yy, 2)):
                        if in_range(kx, ky, kz):
                            add_pair(acc[yy], mine[yy], [side[s, k, n, i] for k in range(3)], limit)
                if in_range(kx, 1, kz):
                    add_pair(cross, inner, [side[s, k, n, 4] for k in range(3)], limit)
            for k in range(3):
                parts[0][k][kz], parts[1][k][kz] = acc[0][k], acc[1][k]
                if cross[k] is not None:
                    parts[2][k][kz] = cross[k]
        for k in range(3):
            zero, one, cross = [row_frame(parts[i][k]) for i in range(3)]
            base[k, x, 0] = zero + jnp.where(lo, 0.0, cross)
            base[k, x, 1] = one + jnp.where(lo, cross, 0.0)


def add_corners(got, frames, table, base, total, upper):
    lo = low_half()
    side, edge, inset = (1, 3, 2) if upper else (0, 0, 1)
    near, deep = [[swap_halves(got[k, i]) for k in range(3)] for i in (0, 2)]
    far = [got[k, 1] for k in range(3)]
    outer_parts, inner_parts, inset_parts = [[{} for _ in range(3)] for _ in range(3)]
    for kz in (-2, -1, 0, 1, 2):
        limit = table[kz + 2, side, 1]
        mine = [[frames[kz + 2, k, edge, yy] for k in range(3)] for yy in range(2)]
        outer = [jnp.where(lo, mine[0][k], mine[1][k]) for k in range(3)]
        inner = [jnp.where(lo, mine[1][k], mine[0][k]) for k in range(3)]
        on_outer, on_inner, on_inset = [None] * 3, [None] * 3, [None] * 3
        add_pair(on_outer, outer, near, limit)
        if in_range(1, 2, kz):
            add_pair(on_outer, outer, far, limit)
            add_pair(on_inner, inner, near, limit)
            add_pair(on_outer, outer, deep, limit)
            mine = [[frames[kz + 2, k, inset, yy] for k in range(3)] for yy in range(2)]
            add_pair(on_inset, [jnp.where(lo, mine[0][k], mine[1][k]) for k in range(3)], near, limit)
        for k in range(3):
            outer_parts[k][kz] = on_outer[k]
            if on_inner[k] is not None:
                inner_parts[k][kz], inset_parts[k][kz] = on_inner[k], on_inset[k]
    total[...] = base[...]
    for k in range(3):
        on_outer, on_inner, on_inset = row_frame(outer_parts[k]), row_frame(inner_parts[k]), row_frame(inset_parts[k])
        total[k, edge, 0] = base[k, edge, 0] + jnp.where(lo, on_outer, on_inner)
        total[k, edge, 1] = base[k, edge, 1] + jnp.where(lo, on_inner, on_outer)
        total[k, inset, 0] = base[k, inset, 0] + jnp.where(lo, on_inset, 0.0)
        total[k, inset, 1] = base[k, inset, 1] + jnp.where(lo, 0.0, on_inset)


def first_corner_kernel(got, frames, table, base, total):
    add_corners(got, frames, table, base, total, False)


def finish_kernel(got, frames, table, base, half, code, vel_out, frc_out, total, new_vel, new_frc, sems):
    add_corners(got, frames, table, base, total, True)
    lo = low_half()
    copies = []
    for k in range(3):
        lattice = total[k].reshape(CELLS, ATOMS)
        flipped = jnp.swapaxes(jnp.concatenate([lattice, lattice], axis=0), 0, 1)
        cells_first = jnp.where(lo[0:1], flipped[:CELLS], flipped[CELLS:])
        for g in range(8):
            rows = slice(g * 8, g * 8 + 8)
            value = lookup(cells_first[rows], code[rows, :])
            new_frc[k, rows, :] = value
            new_vel[k, rows, :] = half[k, rows, :] + (0.5 * TIME_STEP) * value
        leaving = [pltpu.make_async_copy(new_frc.at[k], frc_out.at[k], sems.at[k]),
                   pltpu.make_async_copy(new_vel.at[k], vel_out.at[k], sems.at[3 + k])]
        for copy in leaving:
            copy.start()
        copies += leaving
    for copy in copies:
        copy.wait()


def kernel_call(body, outs, args, specs=None, outs_specs=None, scratch=(), flops=0, name=None):
    moved = sum(4 * a.size for a in args) + sum(4 * s.size for s in outs)
    return pl.pallas_call(
        body,
        out_shape=outs,
        in_specs=[VMEM] * len(args) if specs is None else specs,
        out_specs=[VMEM] * len(outs) if outs_specs is None else outs_specs,
        scratch_shapes=list(scratch),
        compiler_params=pltpu.CompilerParams(vmem_limit_bytes=8 << 20),
        cost_estimate=pl.CostEstimate(flops=flops, bytes_accessed=moved, transcendentals=0),
        name=name,
    )(*args)


def pairing(count, odd):
    if odd:
        return [(i, (i + 1) % count if i % 2 else (i - 1) % count) for i in range(count)]
    return [(i, i ^ 1) for i in range(count)]


def exchange(first, second, axis):
    count = lax.axis_size(axis)
    return (lax.ppermute(first, axis, pairing(count, True)), lax.ppermute(second, axis, pairing(count, False)))


def pass_round(first, second, axis):
    count = lax.axis_size(axis)
    up = [(i, (i + 1) % count) for i in range(count)]
    down = [(target, source) for source, target in up]
    from_lower = lax.ppermute(first, axis, up)
    return lax.ppermute(second, axis, down), from_lower


def per_device(positions, velocities, forces, tiles, counts):
    blocks, _, atoms = positions.shape
    assert blocks == CELLS and atoms == ATOMS
    row_count, col_count = lax.axis_size("row"), lax.axis_size("col")
    assert row_count % 2 == 0 and col_count % 2 == 0 and min(row_count, col_count) > 2
    by_component = [jnp.transpose(a, (1, 0, 2)) for a in (positions, velocities, forces)]
    tile_rows = jnp.transpose(tiles[0, 0], (1, 0))

    def f32(*shape):
        return jax.ShapeDtypeStruct(shape, F32)

    span = f32(3, CELLS, ATOMS)
    lattice = f32(3, 4, 2, 8, ATOMS)
    sums = f32(5, 3, 4, 2, 8, ATOMS)
    moved, half, code, own, mask, pay_a, pay_b, face_a, face_b = kernel_call(
        functools.partial(prepare_kernel, row_count, col_count),
        [span, span, jax.ShapeDtypeStruct((CELLS, ATOMS), jnp.int32), lattice, f32(2, 8, ATOMS),
         f32(14, 8, ATOMS), f32(14, 8, ATOMS), f32(3, 2, 2, 8, ATOMS), f32(3, 2, 2, 8, ATOMS)],
        [*(pltpu.with_memory_space_constraint(a, pltpu.HBM) for a in (*by_component, tile_rows)), counts],
        specs=[HBM, HBM, HBM, HBM, SMEM], name="prepare",
        scratch=[pltpu.VMEM(span.shape, F32)] * 3
        + [pltpu.VMEM(tile_rows.shape, jnp.int32), pltpu.SemaphoreType.DMA((10,))],
    )
    got_a, got_b = exchange(pay_a, pay_b, "col")
    face_a, face_b = pass_round(face_a, face_b, "row")
    frames, total, moved = kernel_call(own_kernel, [sums, sums, span], [own, mask, moved], flops=10**8, name="own",
                                       outs_specs=[VMEM, VMEM, HBM], scratch=[pltpu.SemaphoreType.DMA])
    far_a, far_b = pass_round(
        *kernel_call(relay_kernel, [f32(3, 3, 8, ATOMS)] * 2, [got_a, got_b], name="relay"), "row"
    )
    total, table = kernel_call(
        column_kernel, [sums, f32(5, 2, 2, 8, ATOMS)],
        [own, mask, got_a, got_b, frames, total], flops=10**8, name="column",
        scratch=[pltpu.VMEM((3, 4, 4, 8, ATOMS), F32), pltpu.VMEM((5, 2, 8, ATOMS), F32)],
    )
    (base,) = kernel_call(
        row_kernel, [lattice], [face_a, face_b, frames, total, table], flops=10**8, name="rows",
        scratch=[pltpu.VMEM((2, 3, 2, 5, 8, ATOMS), F32)],
    )
    (base,) = kernel_call(first_corner_kernel, [lattice], [far_b, frames, table, base], flops=10**7, name="corners")
    new_vel, new_frc = kernel_call(
        finish_kernel, [span, span], [far_a, frames, table, base, half, code], flops=10**8,
        name="finish", outs_specs=[HBM, HBM],
        scratch=[pltpu.VMEM(lattice.shape, F32), pltpu.VMEM(span.shape, F32), pltpu.VMEM(span.shape, F32),
                 pltpu.SemaphoreType.DMA((6,))],
    )
    return tuple(jnp.transpose(a, (1, 0, 2)) for a in (moved, new_vel, new_frc))


def solution(mesh):
    in_specs = (
        P(("row", "col"), None, None),
        P(("row", "col"), None, None),
        P(("row", "col"), None, None),
        P("row", "col", None, None),
        P("row", "col"),
    )
    out_specs = (
        P(("row", "col"), None, None),
        P(("row", "col"), None, None),
        P(("row", "col"), None, None),
    )
    return jax.shard_map(
        per_device, mesh=mesh, in_specs=in_specs, out_specs=out_specs, check_vma=False
    )
```

```python
import functools

import jax
import jax.numpy as jnp
from jax import lax
from jax.experimental import pallas as pl
from jax.experimental.pallas import tpu as pltpu
from jax.sharding import PartitionSpec as P


TIME_STEP = 0.01
CUT_SQ = 6.25
SHIFT_FORCE = 24.0 * (2.0 * 2.5 ** (-13) - 2.5 ** (-7))
SPACING = 1.2
CELL_XY = 4.8
CELL_Z = 9.6
CELLS = 64
ATOMS = 128
F32 = jnp.float32
VMEM = pl.BlockSpec(memory_space=pltpu.VMEM)
SMEM = pl.BlockSpec(memory_space=pltpu.SMEM)
HBM = pl.BlockSpec(memory_space=pltpu.HBM)


def lanes():
    return lax.broadcasted_iota(jnp.int32, (8, ATOMS), 1)


def rows8():
    return lax.broadcasted_iota(jnp.int32, (8, ATOMS), 0)


def low_half():
    return lanes() < CELLS


def swap_halves(v):
    return pltpu.roll(v, CELLS, 1)


def from_cell_below(v):
    at_edge = (lanes() & (CELLS - 1)) == 0
    return jnp.where(at_edge, pltpu.roll(v, CELLS + 1, 1), pltpu.roll(v, 1, 1))


def from_cell_above(v):
    at_edge = (lanes() & (CELLS - 1)) == CELLS - 1
    return jnp.where(at_edge, pltpu.roll(v, CELLS - 1, 1), pltpu.roll(v, ATOMS - 1, 1))


def lookup(values, index):
    return jnp.take_along_axis(values, index, axis=1)


def wrapped(step, count):
    step = jnp.where(step < 0, step + count, step)
    return jnp.where(step >= count, step - count, step)


def by_parity(index, pack, first, second):
    odd = (index & 1) == 1

    @pl.when(odd)
    def _():
        pack(first, second)

    @pl.when(jnp.logical_not(odd))
    def _():
        pack(second, first)


def prepare_kernel(row_count, col_count, pos_hbm, vel_hbm, frc_hbm, tiles_hbm, counts,
                   moved_out, half_out, code_out, own_out, mask_out, pay_a, pay_b, face_a, face_b,
                   pos, vel, frc, tiles, sems):
    my_row = lax.axis_index("row")
    my_col = lax.axis_index("col")
    copies = [pltpu.make_async_copy(tiles_hbm, tiles, sems.at[9])]
    for i, (source, target) in enumerate([(pos_hbm, pos), (vel_hbm, vel), (frc_hbm, frc)]):
        for k in range(3):
            copies.append(pltpu.make_async_copy(source.at[k], target.at[k], sems.at[i * 3 + k]))
    for copy in copies[1:4] + copies[:1] + copies[4:]:
        copy.start()
    for copy in copies[1:4]:
        copy.wait()

    place = pos[...]
    lowest = jnp.min(place, axis=2, keepdims=True)
    site = ((place - lowest) * (1.0 / SPACING) + 0.5).astype(jnp.int32)
    code = (site[1] >> 1) * 64 + site[0] * 16 + (site[1] & 1) * 8 + site[2]
    code_out[...] = code

    high, low = code >> 4, code & 15
    number = lax.broadcasted_iota(jnp.int32, (8, ATOMS), 1)
    digit = lax.broadcasted_iota(jnp.int32, (16, ATOMS), 0)
    pick = rows8() * 16 + (lanes() & 15)
    order = []
    for g in range(CELLS // 8):
        rows = slice(g * 8, g * 8 + 8)
        left = [jnp.where(high[rows] == h, number, 0).astype(F32) for h in range(8)]
        right = [jnp.where(digit == low[b : b + 1], 1.0, 0.0).astype(F32) for b in range(g * 8, g * 8 + 8)]
        found = lax.dot_general(
            jnp.concatenate(left, axis=0).astype(jnp.bfloat16), jnp.concatenate(right, axis=0).astype(jnp.bfloat16),
            (((1,), (1,)), ((), ())), preferred_element_type=F32,
        ).astype(jnp.int32)
        atom = lookup(found[:8], pick)
        for h in range(1, 8):
            atom = jnp.where(lanes() >= h * 16, lookup(found[h * 8 : h * 8 + 8], pick), atom)
        order.append(atom)

    for copy in copies[:1] + copies[4:]:
        copy.wait()
    half = vel[...] + (0.5 * TIME_STEP) * frc[...]
    moved = pos[...] + TIME_STEP * half
    half_out[...] = half
    moved_out[...] = moved

    own = []
    for k in range(3):
        cells_first = jnp.concatenate(
            [lookup(moved[k, g * 8 : g * 8 + 8, :], order[g]) for g in range(CELLS // 8)], axis=0
        )
        both = jnp.concatenate([cells_first, pltpu.roll(cells_first, CELLS, 1)], axis=0)
        own.append(jnp.swapaxes(both, 0, 1)[:CELLS].reshape(4, 2, 8, ATOMS))
        own_out[k] = own[k]

    left = tiles[0:1, :]
    right = tiles[1:2, :]
    used = counts[0, 0]
    dx = 2 - wrapped(my_row - (right >> 6) + 1, row_count)
    dy = 2 - wrapped((left >> 6) - my_col + 1, col_count)
    dz = 2 - (((left & 63) - (right & 63) + 1) & 63)
    alive = lax.broadcasted_iota(jnp.int32, left.shape, 1) < used
    kind = jnp.where(alive, dy * 16 + dz * 3 + dx, -1)
    slots = left.shape[1]
    kind_hot = lax.broadcasted_iota(jnp.int32, (48, slots), 0) == kind
    cell_hot = (lax.broadcasted_iota(jnp.int32, (ATOMS, slots), 0) & 63) == (right & 63)
    mask = lax.dot_general(
        jnp.where(kind_hot, 1.0, 0.0).astype(jnp.bfloat16),
        jnp.where(cell_hot, 1.0, 0.0).astype(jnp.bfloat16),
        (((1,), (1,)), ((), ())), preferred_element_type=F32,
    ).reshape(3, 2, 8, ATOMS)
    mask_out[...] = mask[1]

    def pack(to_upper, to_lower):
        lo = low_half()
        for k in range(3):
            for x in range(4):
                first, second = own[k][x, 0], own[k][x, 1]
                up = jnp.where(lo, swap_halves(first), second)
                down = jnp.where(lo, first, swap_halves(second))
                if k == 1:
                    up = up - CELL_XY
                    down = down + CELL_XY
                to_upper[k * 4 + x] = up
                to_lower[k * 4 + x] = down
        to_upper[12:14] = mask[0]
        to_lower[12:14] = mask[2]

    def pack_faces(to_upper, to_lower):
        for k in range(3):
            for yy in range(2):
                for n in range(2):
                    up, down = own[k][2 + n, yy], own[k][n, yy]
                    to_upper[k, n, yy] = up - CELL_XY if k == 0 else up
                    to_lower[k, n, yy] = down + CELL_XY if k == 0 else down

    by_parity(my_col, pack, pay_a, pay_b)
    pack_faces(face_a, face_b)


def row_frames(own, frames):
    for k in range(3):
        for x in range(4):
            for yy in range(2):
                v = own[k, x, yy]
                below = from_cell_below(v)
                above = from_cell_above(v)
                if k == 2:
                    below = below - CELL_Z
                    above = above + CELL_Z
                for kz in (-2, -1, 0, 1, 2):
                    if kz == 0:
                        out = v
                    elif kz > 0:
                        out = pltpu.roll(jnp.where(rows8() >= 8 - kz, below, v), kz, 0)
                    else:
                        out = pltpu.roll(jnp.where(rows8() < -kz, above, v), 8 + kz, 0)
                    frames[kz + 2, k, x, yy] = out


def limits(mask_low, mask_own, mask_high, kz, dx, group):
    def row(mask, dz):
        index = (dz + 1) * 3 + dx + 1
        return jnp.broadcast_to(mask[index // 8, index % 8 : index % 8 + 1, :], (8, ATOMS))

    def both(dz):
        if group == 0:
            return jnp.where(low_half(), row(mask_low, dz), row(mask_own, dz))
        if group == 2:
            return jnp.where(low_half(), row(mask_own, dz), row(mask_high, dz))
        if group == 3:
            return jnp.where(low_half(), row(mask_low, dz), row(mask_high, dz))
        return row(mask_own, dz)

    inner = both(0)
    if kz > 0:
        inner = jnp.where(rows8() < kz, both(1), inner)
    if kz < 0:
        inner = jnp.where(rows8() >= 8 + kz, both(-1), inner)
    return inner * CUT_SQ


def spread(first, second, lower, upper):
    lo = low_half()
    return [
        jnp.where(lo, lower, swap_halves(first)),
        swap_halves(jnp.where(lo, second, lower)),
        first,
        second,
        swap_halves(jnp.where(lo, upper, first)),
        jnp.where(lo, swap_halves(second), upper),
    ]


def pair_weight(mine, theirs):
    away = [mine[k] - theirs[k] for k in range(3)]
    dist = away[0] * away[0] + away[1] * away[1] + away[2] * away[2]
    inv = lax.rsqrt(dist)
    inv_sq = inv * inv
    inv_six = inv_sq * inv_sq * inv_sq
    return away, inv_sq * (inv_six * (48.0 * inv_six - 24.0)) - SHIFT_FORCE * inv, dist


def within(dist, limit):
    return (dist < limit) & (dist > 0.25)


def add_pair(acc, mine, theirs, limit):
    away, weight, dist = pair_weight(mine, theirs)
    weight = jnp.where(within(dist, limit), weight, 0.0)
    for k in range(3):
        term = weight * away[k]
        acc[k] = term if acc[k] is None else acc[k] + term


def in_range(*steps):
    return sum(abs(step) == 2 for step in steps) < 2


def row_frame(parts):
    row = rows8()
    total, above, below = parts.get(0), None, None
    for kz, part in parts.items():
        if kz == 0:
            continue
        back = pltpu.roll(part, (8 - kz) % 8, 0)
        stays = row < 8 - kz if kz > 0 else row >= -kz
        kept, passed = jnp.where(stays, back, 0.0), jnp.where(stays, 0.0, back)
        total = kept if total is None else total + kept
        if kz > 0:
            above = passed if above is None else above + passed
        else:
            below = passed if below is None else below + passed
    if above is not None:
        total = total + from_cell_above(above)
    if below is not None:
        total = total + from_cell_below(below)
    return total


def add_pairs(frames, before, total, partner, limit, columns, rows):
    for kz in (-2, -1, 0, 1, 2):
        for x in range(4):
            for yy in range(2):
                mine = [frames[kz + 2, k, x, yy] for k in range(3)]
                acc = [None if before is None else before[kz + 2, k, x, yy] for k in range(3)]
                for kx in (-2, -1, 0, 1, 2):
                    for ky in (-2, -1, 0, 1, 2):
                        if not in_range(kx, ky, kz):
                            continue
                        if kx == 0 and ky == 0 and kz == 0:
                            continue
                        if x + kx not in columns or yy + ky + 2 not in rows:
                            continue
                        m = yy + ky + 2
                        add_pair(acc, mine, [partner(k, x + kx, m) for k in range(3)],
                                 limit(kz, (x + kx) // 4, m // 2))
                for k in range(3):
                    total[kz + 2, k, x, yy] = jnp.zeros((8, ATOMS), F32) if acc[k] is None else acc[k]


def own_kernel(own, mask, moved, frames, total, moved_out, sem):
    leaving = pltpu.make_async_copy(moved, moved_out, sem)
    leaving.start()
    row_frames(own, frames)
    spots = [(k, x, yy) for k in range(3) for x in range(4) for yy in range(2)]
    home = dict.fromkeys(spots)
    for kz in (1, 2, 0):
        limit = limits(None, mask, None, kz, 0, 1)
        back = limit
        if kz > 0:
            same = jnp.broadcast_to(mask[0, 4:5, :], (8, ATOMS))
            other = from_cell_below(jnp.broadcast_to(mask[0, 1:2, :], (8, ATOMS)))
            back = jnp.where(rows8() < kz, other, same) * CUT_SQ
        for x in range(4):
            for yy in range(2):
                mine = [frames[kz + 2, k, x, yy] for k in range(3)]
                acc = [home[k, x, yy] if kz == 0 else None for k in range(3)]
                for kx in (-2, -1, 0, 1, 2):
                    for ky in (-1, 0, 1):
                        if kz == 0 and (kx, ky) <= (0, 0) or not in_range(kx, ky, kz):
                            continue
                        if x + kx not in range(4) or yy + ky not in range(2):
                            continue
                        theirs = [own[k, x + kx, yy + ky] for k in range(3)]
                        away, weight, dist = pair_weight(mine, theirs)
                        for k in range(3):
                            term = jnp.where(within(dist, limit), weight, 0.0) * away[k]
                            acc[k] = term if acc[k] is None else acc[k] + term
                            term = jnp.where(within(dist, back), weight, 0.0) * away[k]
                            spot = k, x + kx, yy + ky
                            home[spot] = -term if home[spot] is None else home[spot] - term
                for k in range(3):
                    if kz == 0:
                        home[k, x, yy] = acc[k]
                    else:
                        total[kz + 2, k, x, yy] = acc[k]
    for k, x, yy in spots:
        total[2, k, x, yy] = home[k, x, yy]
        total[0, k, x, yy] = jnp.zeros((8, ATOMS), F32)
        total[1, k, x, yy] = jnp.zeros((8, ATOMS), F32)
    leaving.wait()


def relay_kernel(got_a, got_b, pay_a, pay_b):
    col_odd = (lax.axis_index("col") & 1) == 1
    lo = low_half()

    def pack(ref, near, far, offset):
        for k in range(3):
            for x in (near, far):
                from_a, from_b = got_a[k * 4 + x], got_b[k * 4 + x]
                if k == 0:
                    from_a, from_b = from_a + offset, from_b + offset
                lower = jnp.where(col_odd, from_b, from_a)
                upper = jnp.where(col_odd, from_a, from_b)
                ref[k, 0 if x == near else 2] = jnp.where(lo, upper, lower)
                if x == near:
                    ref[k, 1] = jnp.where(lo, lower, upper)

    def both(to_upper, to_lower):
        pack(to_upper, 3, 2, -CELL_XY)
        pack(to_lower, 0, 1, CELL_XY)

    both(pay_a, pay_b)


def column_kernel(own, mask, got_a, got_b, frames, total_in, total, table, near, outer):
    col_odd = (lax.axis_index("col") & 1) == 1
    for k in range(3):
        for x in range(4):
            from_a, from_b = got_a[k * 4 + x], got_b[k * 4 + x]
            lower = jnp.where(col_odd, from_b, from_a)
            upper = jnp.where(col_odd, from_a, from_b)
            six = spread(own[k, x, 0], own[k, x, 1], lower, upper)
            near[k, x, 0] = six[0]
            near[k, x, 1] = six[1]
            near[k, x, 2] = six[4]
            near[k, x, 3] = six[5]
    mask_a, mask_b = got_a[12:14], got_b[12:14]
    mask_low = jnp.where(col_odd, mask_b, mask_a)
    mask_high = jnp.where(col_odd, mask_a, mask_b)
    mask_own = mask[...]
    for kz in (-2, -1, 0, 1, 2):
        for n, dx in enumerate((-1, 1)):
            table[kz + 2, n, 0] = limits(mask_low, mask_own, mask_high, kz, dx, 1)
            table[kz + 2, n, 1] = limits(mask_low, mask_own, mask_high, kz, dx, 3)
        for g in (0, 2):
            outer[kz + 2, g // 2] = limits(mask_low, mask_own, mask_high, kz, 0, g)
    add_pairs(frames, total_in, total, lambda k, x, m: near[k, x, m if m < 2 else m - 2],
              lambda kz, dx, g: outer[kz + 2, g // 2], (0, 1, 2, 3), (0, 1, 4, 5))


def row_kernel(s, face, frames, total_in, table, after, base, side):
    lo = low_half()
    for k in range(3):
        for n in range(2):
            zero, one = face[k, n, 0], face[k, n, 1]
            side[k, n, 0] = zero
            side[k, n, 1] = one
            side[k, n, 2] = swap_halves(zero)
            side[k, n, 3] = swap_halves(one)
            side[k, n, 4] = swap_halves(jnp.where(lo, one, zero))

    for x in (2 * s, 2 * s + 1):
        parts = [[{} for _ in range(3)] for _ in range(3)]
        for kz in (-2, -1, 0, 1, 2):
            mine = [[frames[kz + 2, k, x, yy] for k in range(3)] for yy in range(2)]
            inner = [jnp.where(lo, mine[1][k], mine[0][k]) for k in range(3)]
            acc = [[total_in[kz + 2, k, x, yy] for k in range(3)] for yy in range(2)]
            cross = [None] * 3
            limit = table[kz + 2, s, 0]
            for kx in (-2, -1, 1, 2):
                if 0 <= x + kx < 4:
                    continue
                n = x + kx - 4 if s else x + kx + 2
                for yy in range(2):
                    for i, ky in ((0, -yy), (1, 1 - yy), (2 + yy, 2)):
                        if in_range(kx, ky, kz):
                            add_pair(acc[yy], mine[yy], [side[k, n, i] for k in range(3)], limit)
                if in_range(kx, 1, kz):
                    add_pair(cross, inner, [side[k, n, 4] for k in range(3)], limit)
            for k in range(3):
                parts[0][k][kz], parts[1][k][kz] = acc[0][k], acc[1][k]
                if cross[k] is not None:
                    parts[2][k][kz] = cross[k]
        for k in range(3):
            zero, one, cross = [row_frame(parts[i][k]) for i in range(3)]
            base[k, x - 2 * s, 0] = zero + jnp.where(lo, 0.0, cross)
            base[k, x - 2 * s, 1] = one + jnp.where(lo, cross, 0.0)


def add_corners(got, frames, table, base, total, upper):
    lo = low_half()
    side, edge, inset = (1, 3, 2) if upper else (0, 0, 1)
    near, deep = [[swap_halves(got[k, i]) for k in range(3)] for i in (0, 2)]
    far = [got[k, 1] for k in range(3)]
    outer_parts, inner_parts, inset_parts = [[{} for _ in range(3)] for _ in range(3)]
    for kz in (-2, -1, 0, 1, 2):
        limit = table[kz + 2, side, 1]
        mine = [[frames[kz + 2, k, edge, yy] for k in range(3)] for yy in range(2)]
        outer = [jnp.where(lo, mine[0][k], mine[1][k]) for k in range(3)]
        inner = [jnp.where(lo, mine[1][k], mine[0][k]) for k in range(3)]
        on_outer, on_inner, on_inset = [None] * 3, [None] * 3, [None] * 3
        add_pair(on_outer, outer, near, limit)
        if in_range(1, 2, kz):
            add_pair(on_outer, outer, far, limit)
            add_pair(on_inner, inner, near, limit)
            add_pair(on_outer, outer, deep, limit)
            mine = [[frames[kz + 2, k, inset, yy] for k in range(3)] for yy in range(2)]
            add_pair(on_inset, [jnp.where(lo, mine[0][k], mine[1][k]) for k in range(3)], near, limit)
        for k in range(3):
            outer_parts[k][kz] = on_outer[k]
            if on_inner[k] is not None:
                inner_parts[k][kz], inset_parts[k][kz] = on_inner[k], on_inset[k]
    for k in range(3):
        on_outer, on_inner, on_inset = row_frame(outer_parts[k]), row_frame(inner_parts[k]), row_frame(inset_parts[k])
        for at, zero, one in ((edge, (on_outer, on_inner), (on_inner, on_outer)),
                              (inset, (on_inset, 0.0), (0.0, on_inset))):
            total[k, at - 2 * side, 0] = base[k, at - 2 * side, 0] + jnp.where(lo, *zero)
            total[k, at - 2 * side, 1] = base[k, at - 2 * side, 1] + jnp.where(lo, *one)


def first_corner_kernel(got, frames, table, base, total):
    add_corners(got, frames, table, base, total, False)


def finish_kernel(got, frames, table, base, lower, half, code, vel_out, frc_out, total, new_vel, new_frc, sems):
    add_corners(got, frames, table, base, total, True)
    lo = low_half()
    copies = []
    for k in range(3):
        lattice = jnp.concatenate([lower[k].reshape(32, ATOMS), total[k].reshape(32, ATOMS)], axis=0)
        flipped = jnp.swapaxes(jnp.concatenate([lattice, lattice], axis=0), 0, 1)
        cells_first = jnp.where(lo[0:1], flipped[:CELLS], flipped[CELLS:])
        for g in range(8):
            rows = slice(g * 8, g * 8 + 8)
            value = lookup(cells_first[rows], code[rows, :])
            new_frc[k, rows, :] = value
            new_vel[k, rows, :] = half[k, rows, :] + (0.5 * TIME_STEP) * value
        leaving = [pltpu.make_async_copy(new_frc.at[k], frc_out.at[k], sems.at[k]),
                   pltpu.make_async_copy(new_vel.at[k], vel_out.at[k], sems.at[3 + k])]
        for copy in leaving:
            copy.start()
        copies += leaving
    for copy in copies:
        copy.wait()


def kernel_call(body, outs, args, specs=None, outs_specs=None, scratch=(), flops=0, name=None):
    moved = sum(4 * a.size for a in args) + sum(4 * s.size for s in outs)
    return pl.pallas_call(
        body,
        out_shape=outs,
        in_specs=[VMEM] * len(args) if specs is None else specs,
        out_specs=[VMEM] * len(outs) if outs_specs is None else outs_specs,
        scratch_shapes=list(scratch),
        compiler_params=pltpu.CompilerParams(vmem_limit_bytes=8 << 20),
        cost_estimate=pl.CostEstimate(flops=flops, bytes_accessed=moved, transcendentals=0),
        name=name,
    )(*args)


def pairing(count, odd):
    if odd:
        return [(i, (i + 1) % count if i % 2 else (i - 1) % count) for i in range(count)]
    return [(i, i ^ 1) for i in range(count)]


def exchange(first, second, axis):
    count = lax.axis_size(axis)
    return (lax.ppermute(first, axis, pairing(count, True)), lax.ppermute(second, axis, pairing(count, False)))


def pass_round(first, second, axis):
    count = lax.axis_size(axis)
    up = [(i, (i + 1) % count) for i in range(count)]
    down = [(target, source) for source, target in up]
    from_lower = lax.ppermute(first, axis, up)
    return lax.ppermute(second, axis, down), from_lower


def per_device(positions, velocities, forces, tiles, counts):
    blocks, _, atoms = positions.shape
    assert blocks == CELLS and atoms == ATOMS
    row_count, col_count = lax.axis_size("row"), lax.axis_size("col")
    assert row_count % 2 == 0 and col_count % 2 == 0 and min(row_count, col_count) > 2
    by_component = [jnp.transpose(a, (1, 0, 2)) for a in (positions, velocities, forces)]
    tile_rows = jnp.transpose(tiles[0, 0], (1, 0))

    def f32(*shape):
        return jax.ShapeDtypeStruct(shape, F32)

    span = f32(3, CELLS, ATOMS)
    lattice = f32(3, 4, 2, 8, ATOMS)
    sums = f32(5, 3, 4, 2, 8, ATOMS)
    moved, half, code, own, mask, pay_a, pay_b, face_a, face_b = kernel_call(
        functools.partial(prepare_kernel, row_count, col_count),
        [span, span, jax.ShapeDtypeStruct((CELLS, ATOMS), jnp.int32), lattice, f32(2, 8, ATOMS),
         f32(14, 8, ATOMS), f32(14, 8, ATOMS), f32(3, 2, 2, 8, ATOMS), f32(3, 2, 2, 8, ATOMS)],
        [*(pltpu.with_memory_space_constraint(a, pltpu.HBM) for a in (*by_component, tile_rows)), counts],
        specs=[HBM, HBM, HBM, HBM, SMEM], name="prepare",
        scratch=[pltpu.VMEM(span.shape, F32)] * 3
        + [pltpu.VMEM(tile_rows.shape, jnp.int32), pltpu.SemaphoreType.DMA((10,))],
    )
    got_a, got_b = exchange(pay_a, pay_b, "col")
    face_a, face_b = pass_round(face_a, face_b, "row")
    frames, total, moved = kernel_call(own_kernel, [sums, sums, span], [own, mask, moved], flops=10**8, name="own",
                                       outs_specs=[VMEM, VMEM, HBM], scratch=[pltpu.SemaphoreType.DMA])
    far_a, far_b = pass_round(
        *kernel_call(relay_kernel, [f32(3, 3, 8, ATOMS)] * 2, [got_a, got_b], name="relay"), "row"
    )
    total, table = kernel_call(
        column_kernel, [sums, f32(5, 2, 2, 8, ATOMS)],
        [own, mask, got_a, got_b, frames, total], flops=10**8, name="column",
        scratch=[pltpu.VMEM((3, 4, 4, 8, ATOMS), F32), pltpu.VMEM((5, 2, 8, ATOMS), F32)],
    )
    def rows(side, name, *args):
        return kernel_call(
            functools.partial(row_kernel, side), [f32(3, 2, 2, 8, ATOMS)], args, flops=10**8,
            name=name, scratch=[pltpu.VMEM((3, 2, 5, 8, ATOMS), F32)],
        )[0]

    upper = rows(1, "upper_rows", face_a, frames, total, table, mask)
    lower = rows(0, "lower_rows", face_b, frames, total, table, upper)
    (lower,) = kernel_call(
        first_corner_kernel, [f32(3, 2, 2, 8, ATOMS)], [far_b, frames, table, lower], flops=10**7, name="corners"
    )
    new_vel, new_frc = kernel_call(
        finish_kernel, [span, span], [far_a, frames, table, upper, lower, half, code], flops=10**8,
        name="finish", outs_specs=[HBM, HBM],
        scratch=[pltpu.VMEM((3, 2, 2, 8, ATOMS), F32), pltpu.VMEM(span.shape, F32), pltpu.VMEM(span.shape, F32),
                 pltpu.SemaphoreType.DMA((6,))],
    )
    return tuple(jnp.transpose(a, (1, 0, 2)) for a in (moved, new_vel, new_frc))


def solution(mesh):
    in_specs = (
        P(("row", "col"), None, None),
        P(("row", "col"), None, None),
        P(("row", "col"), None, None),
        P("row", "col", None, None),
        P("row", "col"),
    )
    out_specs = (
        P(("row", "col"), None, None),
        P(("row", "col"), None, None),
        P(("row", "col"), None, None),
    )
    return jax.shard_map(
        per_device, mesh=mesh, in_specs=in_specs, out_specs=out_specs, check_vma=False
    )
```
